768 devices in a mesh: ctx: 96 (over z, y), head: 8 (over x, core).
Axes of the slice: x: 4, y: 8, z: 12, core: 2. Of those that a mesh axis runs over, the one named last changes fastest.
Arguments:
- queries: bfloat16 [12288, 3072], P('ctx', 'head'), may hold values from -6 to 6
- key_vectors: bfloat16 [12288, 3072], P('ctx', 'head'), may hold values from -6 to 6
- value_vectors: bfloat16 [12288, 3072], P('ctx', 'head'), may hold values from -13 to 13
- out_grad: bfloat16 [12288, 3072], P('ctx', 'head'), may hold values from -6 to 6
- log_decay: float32 [32, 12288], P('head', 'ctx'), may hold values from -2 to 0, as said below
- doc_ids: int32 [12288], replicated, may hold values from 0 to 5, never falling along the last dimension, each value on 1 to 4096 neighbouring positions
Outputs:
- attended: bfloat16 [12288, 3072], P('ctx', 'head')
- grad_query: bfloat16 [12288, 3072], P('ctx', 'head')
- grad_key: bfloat16 [12288, 3072], P('ctx', 'head')
- grad_value: bfloat16 [12288, 3072], P('ctx', 'head')
The draws below stay inside these ranges and needn't reach their ends.
Inputs may be any that keep to these rules, and one draw needn't show every extreme that they name: `doc_ids`: ids never fall; each of the 6 documents holds 1 to 4096 tokens, and one holds exactly that many. `log_decay`: strictly negative.
All inputs are finite; a program needn't handle non-finite values.
Results may differ from the reference program's by a relative error of at most 0.0014.
Values sent between devices are 32-bit elements; how exact they have to be, the bound alone decides.
A program may use at most 64 MiB of HBM per device.

```python
import math
import jax
import jax.numpy as jnp
import numpy as np
from jax import lax

HEAD_TOTAL = 32
DH = 96
BLOCK = 128
DOCS = 6
TOK_DEV = 128
TOKENS = 12288


def draw_log_decay(key, part):
    every_key = jax.random.split(key, 7)
    fast_share = 0.5
    fast_heads = jax.random.uniform(every_key[0], (HEAD_TOTAL, 1)) < fast_share
    fast_rate = jnp.exp(jax.random.uniform(every_key[1], (HEAD_TOTAL, 1), minval=math.log(1.0 / 50.0), maxval=math.log(1.0 / 30.0)))
    slow_rate = jax.random.uniform(every_key[2], (HEAD_TOTAL, 1), minval=0.05, maxval=0.3) * math.log(10.0) / TOKENS
    decay_speed = jnp.where(fast_heads, fast_rate, slow_rate)
    device_multiple = jnp.exp(jax.random.uniform(every_key[3], (HEAD_TOTAL, TOKENS // TOK_DEV, 1), minval=math.log(0.5), maxval=math.log(2.0)))
    device_multiple = jnp.broadcast_to(device_multiple, (HEAD_TOTAL, TOKENS // TOK_DEV, TOK_DEV)).reshape(HEAD_TOTAL, TOKENS)
    token_multiple = jnp.exp(jax.random.uniform(every_key[4], (HEAD_TOTAL, TOKENS), minval=math.log(0.5), maxval=math.log(2.0)))
    positions = jax.random.randint(every_key[5], (2,), 0, TOKENS)
    hop_depth = jax.random.uniform(every_key[6], (HEAD_TOTAL, 2), minval=math.log(0.5), maxval=math.log(0.8))
    index_row = jnp.arange(TOKENS, dtype=jnp.int32)
    match_table = (index_row[None, None, :] == positions[None, :, None]).astype(jnp.float32)
    hop_rounds = jnp.sum(match_table * hop_depth[:, :, None], axis=1)
    return (hop_rounds - decay_speed * device_multiple * token_multiple).astype(jnp.float32)


def draw_value_vectors(key, part):
    every_key = jax.random.split(key, 2)
    base_values = jnp.clip(jax.random.normal(every_key[0], (TOKENS, HEAD_TOTAL * DH)), -6.0, 6.0)
    rise_span = 0.5 * math.log(3.0)
    head_place = jnp.arange(HEAD_TOTAL, dtype=jnp.float32) / max(HEAD_TOTAL - 1, 1)
    jitter = jax.random.uniform(every_key[1], (HEAD_TOTAL,), minval=-0.2, maxval=0.2)
    head_scale = jnp.exp(rise_span * head_place + jitter)
    column_scale = jnp.repeat(head_scale, DH)
    return (base_values * column_scale[None, :]).astype(jnp.bfloat16)


def level_of(rng, dims, pieces, smallest, high):
    level = 1.0
    for position, shards_of in pieces:
        steps = jax.random.uniform(jax.random.fold_in(jax.random.fold_in(rng, 6), position), (shards_of,), jnp.float32, smallest / len(pieces), high / len(pieces))
        level = level * jnp.repeat(jnp.exp(steps), dims[position] // shards_of).reshape((-1,) + (1,) * (len(dims) - 1 - position))
    return level


def split_up(amount, total, bound, slope):
    loads = [(1 << 20) // math.isqrt(rank ** slope) + 1 for rank in range(2, amount + 1)]
    spare, counts = total - bound - (amount - 1), [1] * (amount - 1)
    while spare > 0:
        movable = [i for i in range(amount - 1) if counts[i] < bound]
        mass, budget = sum([loads[i] for i in movable]), spare
        for i in movable:
            extra = min(bound - counts[i], max(1, budget * loads[i] // mass), spare)
            counts[i] = counts[i] + extra
            spare = spare - extra
    return np.array([bound] + counts)


def ragged(own_key, count, total, most, skew):
    if count == 2:
        one = jax.random.randint(own_key, (), max(1, total - most), min(most, total - 1) + 1)
        return jnp.stack([one, total - one])
    lengths = jnp.asarray(split_up(count, total, most, skew), jnp.int32)
    twos = (count - 1) // 2
    source_of, receiver = lengths[1:1 + 2 * twos:2], lengths[2:2 + 2 * twos:2]
    slack = jnp.minimum(source_of - 1, most - receiver)
    shifted = jax.random.randint(jax.random.fold_in(own_key, 1), (twos,), 0, 1 << 20) % (slack + 1)
    lengths = lengths.at[1:1 + 2 * twos:2].set(source_of - shifted).at[2:2 + 2 * twos:2].set(receiver + shifted)
    return lengths[jax.random.permutation(jax.random.fold_in(own_key, 2), count)]


def normal_values(own_key, extent, deviation, limit, cuts=(), kind=jnp.bfloat16):
    entries = deviation * jax.random.normal(own_key, extent, jnp.float32)
    if cuts:
        entries = entries * level_of(own_key, extent, cuts, -0.22, 0.18)
    return jnp.clip(entries, -limit, limit).astype(kind)


def setup_inputs(seed: int = 0) -> dict:
    key_of = jax.random.split(jax.random.key(seed), 7)
    return {
        "queries": normal_values(key_of[0], (TOKENS, HEAD_TOTAL * DH), 1.0, 6.0, ((0, 96), (1, 8))),
        "key_vectors": normal_values(key_of[1], (TOKENS, HEAD_TOTAL * DH), 1.0, 6.0, ((0, 96), (1, 8))),
        "value_vectors": draw_value_vectors(jax.random.fold_in(key_of[6], 71), 0),
        "out_grad": normal_values(key_of[3], (TOKENS, HEAD_TOTAL * DH), 1.0, 6.0, ((0, 96), (1, 8))),
        "log_decay": draw_log_decay(jax.random.fold_in(key_of[6], 71), 0),
        "doc_ids": jnp.searchsorted(jnp.cumsum(ragged(key_of[5], DOCS, TOKENS, TOKENS // 3, 0)), jnp.arange(TOKENS), side="right").astype(jnp.int32),
    }


highest = lax.Precision.HIGHEST
epsilon = 1e-05

def contract(pattern, operand_one, operand_two):
    return jnp.einsum(pattern, operand_one, operand_two, precision=highest)

def block_weights(log_rates, doc_block, before):
    cumulative = jnp.cumsum(log_rates, axis=1)
    spread = cumulative[:, :, None] - cumulative[:, None, :]
    length = doc_block.shape[0]
    row_index = lax.broadcasted_iota(jnp.int32, (length, length), 0)
    col_index = lax.broadcasted_iota(jnp.int32, (length, length), 1)
    inside = (row_index >= col_index) & (doc_block[:, None] == doc_block[None, :])
    within = jnp.exp(jnp.minimum(spread, 0.0)) * inside.astype(jnp.float32)[None]
    carried = (doc_block == before).astype(jnp.float32)
    entering = jnp.exp(cumulative) * carried[None, :]
    final_sum = cumulative[:, -1:]
    leaving = jnp.exp(final_sum - cumulative) * (doc_block == doc_block[-1]).astype(jnp.float32)[None, :]
    passing = jnp.exp(final_sum[:, 0]) * carried[-1]
    return (within, entering, leaving, passing)

def block_forward(scaled, key_now, value_now, carry_state, weights):
    within, entering, leaving, passing = weights
    scores = contract('thd,shd->hts', scaled, key_now)
    local_part = contract('hts,shd->thd', within * scores, value_now)
    carried = contract('thd,hde->the', scaled, carry_state) * entering.T[:, :, None]
    update = contract('shd,she->hde', key_now * leaving.T[:, :, None], value_now)
    return (local_part + carried, passing[:, None, None] * carry_state + update)

def reference(queries, key_vectors, value_vectors, out_grad, log_decay, doc_ids):
    blocks = TOKENS // BLOCK
    group_size = math.gcd(HEAD_TOTAL, 8)
    group_count = HEAD_TOTAL // group_size
    factor = DH ** (-0.5)
    full_width = HEAD_TOTAL * DH
    doc_blocks = doc_ids.reshape(blocks, BLOCK)
    previous = jnp.concatenate([jnp.full((1,), -1, jnp.int32), doc_blocks[:-1, -1]])

    def unfold(source_array, group_index):
        column = (group_index * group_size * DH).astype(jnp.int32)
        piece_cols = lax.dynamic_slice_in_dim(source_array, column, group_size * DH, 1)
        return piece_cols.astype(jnp.float32).reshape(blocks, BLOCK, group_size, DH)

    def weights_of(group_index):
        rate_rows = lax.dynamic_slice_in_dim(log_decay, (group_index * group_size).astype(jnp.int32), group_size, 0)
        rate_rows = rate_rows.reshape(group_size, blocks, BLOCK).transpose(1, 0, 2)
        return jax.vmap(block_weights)(rate_rows, doc_blocks, previous)

    def raw_forward(weights, query_all, key_all, value_all):

        def advance(carry_state, inputs_now):
            query_now, key_now, value_now, weight_now = inputs_now
            out_now, carry_state = block_forward(query_now * factor, key_now, value_now, carry_state, weight_now)
            return (carry_state, out_now)
        start_state = jnp.zeros((group_size, DH, DH), jnp.float32)
        ignored, outputs = lax.scan(advance, start_state, (query_all, key_all, value_all, weights))
        return outputs

    def forward_pass(group_index):
        return raw_forward(weights_of(group_index), unfold(queries, group_index), unfold(key_vectors, group_index), unfold(value_vectors, group_index))
    indices = jnp.arange(group_count, dtype=jnp.int32)
    raw_all = lax.map(forward_pass, indices)
    squares = lax.optimization_barrier(jnp.sum(raw_all * raw_all, axis=(0, 3, 4)))

    def dot_pass(group_index):
        return lax.optimization_barrier(jnp.sum(raw_all[group_index] * unfold(out_grad, group_index), axis=(2, 3)))
    dots = lax.optimization_barrier(jnp.sum(lax.map(dot_pass, indices), axis=0))
    rscale = lax.rsqrt(squares / full_width + epsilon)
    drift = rscale * rscale * rscale * dots / full_width

    def backward_pass(group_index):
        raw_now = raw_all[group_index]
        grad_raw = rscale[:, :, None, None] * unfold(out_grad, group_index) - raw_now * drift[:, :, None, None]
        normed = raw_now * rscale[:, :, None, None]
        weights = weights_of(group_index)

        def closed(query_all, key_all, value_all):
            return raw_forward(weights, query_all, key_all, value_all)
        ignored, pullback = jax.vjp(closed, unfold(queries, group_index), unfold(key_vectors, group_index), unfold(value_vectors, group_index))
        pulled = pullback(grad_raw)
        return (normed.astype(jnp.bfloat16), pulled[0].astype(jnp.bfloat16), pulled[1].astype(jnp.bfloat16), pulled[2].astype(jnp.bfloat16))
    results = lax.map(backward_pass, indices)

    def fold_rows(source_array):
        return source_array.transpose(1, 2, 0, 3, 4).reshape(TOKENS, HEAD_TOTAL * DH)
    return (fold_rows(results[0]), fold_rows(results[1]), fold_rows(results[2]), fold_rows(results[3]))
```

```python
import jax
import jax.numpy as jnp
from jax import lax
from jax.experimental import pallas as pl
from jax.experimental.pallas import tpu as pltpu
from jax.sharding import PartitionSpec as P

HEADS = 4
DH = 96
TOK = 128
WIDTH = HEADS * DH
FULL = 3072
ROW = 8
ROWS = 12
HEAD_DEVS = 8
HALF = DH // 2
EPS = 1e-05
FACTOR = DH ** (-0.5)
F32 = jnp.float32
BF16 = jnp.bfloat16
MESH = pl.DeviceIdType.MESH


def nn(a, b):
    return lax.dot_general(a, b, (((1,), (0,)), ((), ())), preferred_element_type=F32)


def nt(a, b):
    return lax.dot_general(a, b, (((1,), (1,)), ((), ())), preferred_element_type=F32)


def split(x):
    hi = x.astype(BF16)
    return hi, (x - hi.astype(F32)).astype(BF16)


def two(dot, a, b):
    return dot(a[0], b) + dot(a[1], b)


def two_right(dot, a, b):
    return dot(a, b[0]) + dot(a, b[1])


def three(dot, a, b):
    return dot(a[0], b[0]) + (dot(a[0], b[1]) + dot(a[1], b[0]))


def kernel(
    q_ref, k_ref, v_ref, g_ref, ld_ref, doc_ref,
    att_ref, dq_ref, dk_ref, dv_ref,
    qh, kh, vh, gh, qt, within, score, ent, leave, out, state_hi, state_lo,
    out_hi, out_lo, dkl, dvl,
    up, up_in, part, back, back_in, zout, zin,
    upb, upb_in, partb, backb, backb_in, zoutb, zinb,
    hsend, hrecv,
    a_send, a_recv, z_send, z_recv, h_send, h_recv,
):
    ctx = lax.axis_index("ctx")
    head = lax.axis_index("head")
    y = lax.rem(ctx, ROW)
    z = ctx // ROW

    def at_row(step):
        return lax.rem(z + step + ROWS, ROWS) * ROW + y

    barrier = pltpu.get_barrier_semaphore()
    for step in range(1, ROW):
        pl.semaphore_signal(
            barrier, inc=1, device_id=(z * ROW + lax.rem(y + step, ROW), head), device_id_type=MESH
        )
    for step in (-2, -1, 1, 2):
        pl.semaphore_signal(barrier, inc=1, device_id=(at_row(step), head), device_id_type=MESH)
    for step in range(1, HEAD_DEVS):
        pl.semaphore_signal(
            barrier, inc=1, device_id=(ctx, lax.rem(head + step, HEAD_DEVS)), device_id_type=MESH
        )

    lane = lax.broadcasted_iota(jnp.int32, (TOK, TOK), 1)
    sub = lax.broadcasted_iota(jnp.int32, (TOK, TOK), 0)
    real = lane < DH
    real_half = lax.broadcasted_iota(jnp.int32, (HALF, TOK), 1) < DH

    def heads_of(ref):
        tiles = [ref[:, TOK * t : TOK * t + TOK].astype(F32) for t in range(3)]
        zero = jnp.zeros((TOK, TOK), F32)
        h0 = tiles[0]
        h1 = pltpu.roll(jnp.where(lane >= 96, tiles[0], tiles[1]), 32, 1)
        h2 = pltpu.roll(jnp.where(lane >= 64, tiles[1], tiles[2]), 64, 1)
        h3 = pltpu.roll(tiles[2], 96, 1)
        return [jnp.where(real, h, zero) for h in (h0, h1, h2, h3)]

    def put_heads(ref, parts):
        r1 = pltpu.roll(parts[1], 96, 1)
        r2 = pltpu.roll(parts[2], 64, 1)
        r3 = pltpu.roll(parts[3], 32, 1)
        ref[:, 0:TOK] = jnp.where(lane < 96, parts[0], r1).astype(BF16)
        ref[:, TOK : 2 * TOK] = jnp.where(lane < 64, r1, r2).astype(BF16)
        ref[:, 2 * TOK : 3 * TOK] = jnp.where(lane < 32, r2, r3).astype(BF16)

    def spread(row):
        return jnp.transpose(jnp.broadcast_to(row, (TOK, TOK)))

    upper = (sub <= lane).astype(F32)
    sums = lax.dot_general(
        ld_ref[...], upper, (((1,), (0,)), ((), ())),
        precision=lax.Precision.HIGHEST, preferred_element_type=F32,
    )
    doc_row = doc_ref[pl.ds(ctx, 1), :].astype(F32)
    earlier = doc_ref[pl.ds(jnp.maximum(ctx - 1, 0), 1), :].astype(F32)[:, TOK - 1 : TOK]
    before = jnp.where(ctx > 0, earlier, -1.0)
    last = doc_row[:, TOK - 1 : TOK]
    enter_row = (doc_row == before).astype(F32)
    leave_row = (doc_row == last).astype(F32)
    through = (last == before).astype(F32)
    doc_col = spread(doc_row)
    inside = (sub >= lane) & (doc_col == doc_row)
    enter_col = (doc_col == before).astype(F32)
    leave_col = (doc_col == last).astype(F32)

    k_heads = heads_of(k_ref)
    v_heads = heads_of(v_ref)
    passing = []
    for h in range(HEADS):
        row = sums[h : h + 1, :]
        final = row[:, TOK - 1 : TOK]
        passing.append(jnp.exp(final) * through)
        vb = v_heads[h].astype(BF16)
        vh[h] = vb
        kh[h] = k_heads[h].astype(BF16)
        kt = jnp.transpose(k_heads[h]) * (jnp.exp(final - row) * leave_row)
        update = two(nn, split(kt), vb)
        tile = jnp.where(real, update, passing[h])
        up[2 * h] = tile[0:HALF]
        up[2 * h + 1] = tile[HALF:DH]

    pl.semaphore_wait(barrier, (ROW - 1) + 4 + (HEAD_DEVS - 1))

    def remote(src, dst, send_sem, recv_sem, target):
        return pltpu.make_async_remote_copy(
            src_ref=src, dst_ref=dst, send_sem=send_sem, recv_sem=recv_sem,
            device_id=target, device_id_type=MESH,
        )

    def across(phase, src, dst):
        copies = []
        for step in range(1, ROW):
            other = lax.rem(y + step, ROW)
            copy = remote(
                src.at[other], dst.at[y], a_send.at[phase, step], a_recv.at[phase, y],
                (z * ROW + other, head),
            )
            copy.start()
            copies.append(copy)
        dst[pl.ds(y, 1)] = src[pl.ds(y, 1)]
        return copies

    def arrive(phase, dst):
        for step in range(1, ROW):
            other = lax.rem(y + step, ROW)
            remote(
                dst.at[other], dst.at[other], a_send.at[phase, step], a_recv.at[phase, other],
                (z * ROW + other, head),
            ).wait_recv()

    def factor_of(tile):
        return jnp.broadcast_to(tile[:, DH : DH + 1], tile.shape)

    def join(near, far):
        return jnp.where(real_half, near, 0.0) + factor_of(near) * far

    def row_scan(base, forward, arrived, prefix, zo, zi, result):
        arrive(base, arrived)
        order = range(ROW) if forward else range(ROW - 1, -1, -1)
        running = jnp.where(real_half, 0.0, 1.0)
        for place in order:
            prefix[place] = running
            running = join(arrived[place], running)
        zo[0] = running
        sign = 1 if forward else -1
        sends = []
        for n, (slot, step) in enumerate(((0, sign), (0, 2 * sign))):
            copy = remote(
                zo.at[slot], zi.at[n], z_send.at[base, n], z_recv.at[base, n], (at_row(step), head)
            )
            copy.start()
            sends.append(copy)
        sends[0].wait_recv()
        sends[1].wait_recv()
        pair = join(zi[0], zi[1])
        zo[1] = pair
        copy = remote(
            zo.at[1], zi.at[2], z_send.at[base, 2], z_recv.at[base, 2], (at_row(2 * sign), head)
        )
        copy.start()
        sends.append(copy)
        copy.wait_recv()
        entry = pair + factor_of(pair) * zi[2]
        for place in range(ROW):
            tile = prefix[place]
            result[place] = tile + factor_of(tile) * entry
        return sends

    def state_of(arrived, h):
        tile = jnp.concatenate(
            [arrived[2 * h], arrived[2 * h + 1], jnp.zeros((TOK - DH, TOK), F32)], axis=0
        )
        return jnp.where(real, tile, 0.0)

    pending = across(0, up, up_in)

    q_heads = heads_of(q_ref)
    g_heads = heads_of(g_ref)
    for h in range(HEADS):
        row = sums[h : h + 1, :]
        final = row[:, TOK - 1 : TOK]
        col = spread(row)
        qb = q_heads[h].astype(BF16)
        qh[h] = qb
        gh[h] = g_heads[h].astype(BF16)
        qt[h] = jnp.transpose(q_heads[h]) * (jnp.exp(row) * enter_row * FACTOR)
        ent[h] = jnp.exp(col) * enter_col * FACTOR
        leave[h] = jnp.exp(final - col) * leave_col
        weight = jnp.where(inside, jnp.exp(jnp.minimum(col - row, 0.0)), 0.0)
        within[h] = weight
        scores = weight * (nt(qb, kh[h]) * FACTOR)
        score[h] = scores
        out[h] = two(nn, split(scores), vh[h])

    pending += row_scan(0, True, up_in, part, zout, zin, back)
    pending += across(1, back, back_in)
    arrive(1, back_in)

    squares = jnp.zeros((TOK, TOK), F32)
    dots = jnp.zeros((TOK, TOK), F32)
    for h in range(HEADS):
        pair = split(state_of(back_in, h))
        state_hi[h] = pair[0]
        state_lo[h] = pair[1]
        now = out[h] + ent[h] * two_right(nn, qh[h], pair)
        out[h] = now
        squares = squares + now * now
        dots = dots + now * gh[h].astype(F32)
    square_row = jnp.sum(jnp.transpose(squares), axis=0, keepdims=True)
    dot_row = jnp.sum(jnp.transpose(dots), axis=0, keepdims=True)
    small = lax.broadcasted_iota(jnp.int32, (8, TOK), 0)
    tile = jnp.where(small == 0, square_row, dot_row)
    hsend[...] = tile
    for step in range(1, HEAD_DEVS):
        other = lax.rem(head + step, HEAD_DEVS)
        copy = remote(hsend, hrecv.at[head], h_send.at[step], h_recv.at[head], (ctx, other))
        copy.start()
        pending.append(copy)
    hrecv[pl.ds(head, 1)] = tile[None]
    for h in range(HEADS):
        pair = split(out[h])
        out_hi[h] = pair[0]
        out_lo[h] = pair[1]
    for step in range(1, HEAD_DEVS):
        other = lax.rem(head + step, HEAD_DEVS)
        remote(
            hrecv.at[other], hrecv.at[other], h_send.at[step], h_recv.at[other], (ctx, other)
        ).wait_recv()
    total = hrecv[0]
    for slot in range(1, HEAD_DEVS):
        total = total + hrecv[slot]
    rscale = lax.rsqrt(total[0:1] / FULL + EPS)
    drift = rscale * rscale * rscale * total[1:2] / FULL

    for h in range(HEADS):
        near = split(qt[h] * rscale)
        far = split(qt[h] * drift)
        pulled = two(nn, near, gh[h]) - three(nn, far, (out_hi[h], out_lo[h]))
        tile = jnp.where(real, pulled, passing[h])
        upb[2 * h] = tile[0:HALF]
        upb[2 * h + 1] = tile[HALF:DH]

    pending += across(2, upb, upb_in)

    rscale_col = spread(rscale)
    drift_col = spread(drift)
    normed = []
    grads = []
    for h in range(HEADS):
        now = out[h]
        normed.append(now * rscale_col)
        grad_pair = split(rscale_col * gh[h].astype(F32) - drift_col * now)
        mixed = within[h] * two(nt, grad_pair, vh[h])
        grads.append(
            FACTOR * two(nn, split(mixed), kh[h])
            + ent[h] * three(nt, grad_pair, (state_hi[h], state_lo[h]))
        )
        dkl[h] = FACTOR * two(nn, split(jnp.transpose(mixed)), qh[h])
        dvl[h] = three(nn, split(jnp.transpose(score[h])), grad_pair)
    put_heads(att_ref, normed)
    put_heads(dq_ref, grads)

    pending += row_scan(1 + 1, False, upb_in, partb, zoutb, zinb, backb)
    pending += across(3, backb, backb_in)
    arrive(3, backb_in)

    grad_keys = []
    grad_values = []
    for h in range(HEADS):
        pair = split(state_of(backb_in, h))
        grad_keys.append(dkl[h] + leave[h] * two_right(nt, vh[h], pair))
        grad_values.append(dvl[h] + leave[h] * two_right(nn, kh[h], pair))
    put_heads(dk_ref, grad_keys)
    put_heads(dv_ref, grad_values)

    for copy in pending:
        copy.wait_send()


def local(queries, key_vectors, value_vectors, out_grad, log_decay, doc_ids):
    vmem = pl.BlockSpec(memory_space=pltpu.VMEM)
    square_bf = pltpu.VMEM((HEADS, TOK, TOK), BF16)
    square_f = pltpu.VMEM((HEADS, TOK, TOK), F32)
    slices = pltpu.VMEM((ROW, HALF, TOK), F32)
    scan = [slices] * 5 + [pltpu.VMEM((2, HALF, TOK), F32), pltpu.VMEM((3, HALF, TOK), F32)]
    dma = pltpu.SemaphoreType.DMA
    result = jax.ShapeDtypeStruct((TOK, WIDTH), BF16)
    return pl.pallas_call(
        kernel,
        out_shape=[result] * 4,
        in_specs=[vmem] * 6,
        out_specs=[vmem] * 4,
        scratch_shapes=[square_bf] * 4
        + [square_f] * 6
        + [square_bf] * 4
        + [square_f] * 2
        + scan * 2
        + [pltpu.VMEM((8, TOK), F32), pltpu.VMEM((HEAD_DEVS, 8, TOK), F32)]
        + [dma((4, ROW)), dma((4, ROW)), dma((4, 3)), dma((4, 3)), dma((8,)), dma((8,))],
        compiler_params=pltpu.CompilerParams(
            collective_id=0, has_side_effects=True, vmem_limit_bytes=32 << 20
        ),
    )(
        queries, key_vectors, value_vectors, out_grad, log_decay,
        doc_ids.reshape(ROW * ROWS, TOK),
    )


def solution(mesh):
    return jax.shard_map(
        local,
        mesh=mesh,
        in_specs=(
            P("ctx", "head"), P("ctx", "head"), P("ctx", "head"), P("ctx", "head"),
            P("head", "ctx"), P(),
        ),
        out_specs=(P("ctx", "head"),) * 4,
        check_vma=False,
    )
```

```python
import jax
import jax.numpy as jnp
from jax import lax
from jax.experimental import pallas as pl
from jax.experimental.pallas import tpu as pltpu
from jax.sharding import PartitionSpec as P

HEADS = 4
DH = 96
TOK = 128
WIDTH = HEADS * DH
FULL = 3072
ROW = 8
ROWS = 12
HEAD_DEVS = 8
PART = 40
ORDER = (4, 3, 5, 2, 6, 1, 7)
EPS = 1e-05
FACTOR = DH ** (-0.5)
F32 = jnp.float32
BF16 = jnp.bfloat16
MESH = pl.DeviceIdType.MESH


def nn(a, b):
    return lax.dot_general(a, b, (((1,), (0,)), ((), ())), preferred_element_type=F32)


def nt(a, b):
    return lax.dot_general(a, b, (((1,), (1,)), ((), ())), preferred_element_type=F32)


def split(x):
    hi = x.astype(BF16)
    return hi, (x - hi.astype(F32)).astype(BF16)


def two(dot, a, b):
    return dot(a[0], b) + dot(a[1], b)


def two_right(dot, a, b):
    return dot(a, b[0]) + dot(a, b[1])


def three(dot, a, b):
    return dot(a[0], b[0]) + (dot(a[0], b[1]) + dot(a[1], b[0]))


def kernel(
    q_hbm, k_hbm, v_hbm, g_hbm, ld_hbm, doc_hbm,
    att_hbm, dq_hbm, dk_hbm, dv_hbm,
    att_ref, dq_ref, dk_ref, dv_ref, out_sem,
    q_ref, k_ref, v_ref, g_ref, ld_ref, doc_ref, in_sem,
    qh, kh, vh, gh, qt, within, score, ent, leave, out, state_hi, state_lo,
    out_hi, out_lo, dkl, dvl,
    up, up_in, part, back, back_in, zout, zin,
    upb, upb_in, partb, backb, backb_in, zoutb, zinb,
    hsend, hrecv,
    a_send, a_recv, z_send, z_recv, h_send, h_recv,
):
    ctx = lax.axis_index("ctx")
    head = lax.axis_index("head")
    y = lax.rem(ctx, ROW)
    z = ctx // ROW

    def at_row(step):
        return lax.rem(z + step + ROWS, ROWS) * ROW + y

    barrier = pltpu.get_barrier_semaphore()
    for step in range(1, ROW):
        pl.semaphore_signal(
            barrier, inc=1, device_id=(z * ROW + lax.rem(y + step, ROW), head), device_id_type=MESH
        )
    for step in (-2, -1, 1, 2):
        pl.semaphore_signal(barrier, inc=1, device_id=(at_row(step), head), device_id_type=MESH)
    for step in range(1, HEAD_DEVS):
        pl.semaphore_signal(
            barrier, inc=1, device_id=(ctx, lax.rem(head + step, HEAD_DEVS)), device_id_type=MESH
        )

    loads = [
        pltpu.make_async_copy(src, dst, in_sem.at[n])
        for n, (src, dst) in enumerate((
            (ld_hbm, ld_ref), (doc_hbm, doc_ref), (k_hbm, k_ref),
            (v_hbm, v_ref), (q_hbm, q_ref), (g_hbm, g_ref),
        ))
    ]
    for load in loads:
        load.start()

    lane = lax.broadcasted_iota(jnp.int32, (TOK, TOK), 1)
    sub = lax.broadcasted_iota(jnp.int32, (TOK, TOK), 0)
    real = lane < DH
    odd = lax.rem(y, 2)
    part_sub = lax.broadcasted_iota(jnp.int32, (PART, TOK), 0)
    data = (part_sub < 32) | (part_sub // 4 == 8 + odd)
    wide = lax.broadcasted_iota(jnp.int32, (72, TOK), 1) < DH
    third = lax.broadcasted_iota(jnp.int32, (24, TOK), 1)
    low = lax.broadcasted_iota(jnp.int32, (8, TOK), 0) < 4

    def heads_of(ref):
        tiles = [ref[:, TOK * t : TOK * t + TOK].astype(F32) for t in range(3)]
        zero = jnp.zeros((TOK, TOK), F32)
        h0 = tiles[0]
        h1 = pltpu.roll(jnp.where(lane >= 96, tiles[0], tiles[1]), 32, 1)
        h2 = pltpu.roll(jnp.where(lane >= 64, tiles[1], tiles[2]), 64, 1)
        h3 = pltpu.roll(tiles[2], 96, 1)
        return [jnp.where(real, h, zero) for h in (h0, h1, h2, h3)]

    def put_heads(ref, parts):
        r1 = pltpu.roll(parts[1], 96, 1)
        r2 = pltpu.roll(parts[2], 64, 1)
        r3 = pltpu.roll(parts[3], 32, 1)
        ref[:, 0:TOK] = jnp.where(lane < 96, parts[0], r1).astype(BF16)
        ref[:, TOK : 2 * TOK] = jnp.where(lane < 64, r1, r2).astype(BF16)
        ref[:, 2 * TOK : 3 * TOK] = jnp.where(lane < 32, r2, r3).astype(BF16)

    def spread(row):
        return jnp.transpose(jnp.broadcast_to(row, (TOK, TOK)))

    loads[0].wait()
    loads[1].wait()
    upper = (sub <= lane).astype(F32)
    sums = lax.dot_general(
        ld_ref[...], upper, (((1,), (0,)), ((), ())),
        precision=lax.Precision.HIGHEST, preferred_element_type=F32,
    )
    doc_row = doc_ref[pl.ds(ctx, 1), :].astype(F32)
    earlier = doc_ref[pl.ds(jnp.maximum(ctx - 1, 0), 1), :].astype(F32)[:, TOK - 1 : TOK]
    before = jnp.where(ctx > 0, earlier, -1.0)
    last = doc_row[:, TOK - 1 : TOK]
    enter_row = (doc_row == before).astype(F32)
    leave_row = (doc_row == last).astype(F32)
    through = (last == before).astype(F32)
    doc_col = spread(doc_row)
    inside = (sub >= lane) & (doc_col == doc_row)
    enter_col = (doc_col == before).astype(F32)
    leave_col = (doc_col == last).astype(F32)

    def pack(state, decay, slot, dest):
        tail = state[72:96]
        rest = jnp.concatenate(
            [pltpu.roll(tail, 96, 1), pltpu.roll(tail, 64, 1), pltpu.roll(tail, 32, 1)], axis=0
        )
        full = jnp.where(wide, state[0:72], rest)
        dest[slot, 0:32] = full[0:32]
        dest[slot, 32:40] = jnp.where(low, full[32:40], decay)
        dest[slot + 1, 0:32] = full[40:72]
        dest[slot + 1, 32:40] = jnp.where(low, decay, full[32:40])

    def unpack(arrived, h):
        one, other = arrived[2 * h], arrived[2 * h + 1]
        full = jnp.concatenate(
            [one[0:32], jnp.where(low, one[32:40], other[32:40]), other[0:32]], axis=0
        )
        tail = jnp.where(
            third < 32, pltpu.roll(full[0:24], 32, 1),
            jnp.where(third < 64, pltpu.roll(full[24:48], 64, 1), pltpu.roll(full[48:72], 96, 1)),
        )
        tail = jnp.where(third < DH, tail, 0.0)
        return jnp.concatenate(
            [jnp.where(wide, full, 0.0), tail, jnp.zeros((TOK - DH, TOK), F32)], axis=0
        )

    loads[2].wait()
    loads[3].wait()
    k_heads = heads_of(k_ref)
    v_heads = heads_of(v_ref)
    passing = []
    for h in range(HEADS):
        row = sums[h : h + 1, :]
        final = row[:, TOK - 1 : TOK]
        passing.append(jnp.exp(final) * through)
        vb = v_heads[h].astype(BF16)
        vh[h] = vb
        kh[h] = k_heads[h].astype(BF16)
        kt = jnp.transpose(k_heads[h]) * (jnp.exp(final - row) * leave_row)
        update = two(nn, split(kt), vb)
        pack(update, passing[h], 2 * h, up)

    pl.semaphore_wait(barrier, (ROW - 1) + 4 + (HEAD_DEVS - 1))

    def remote(src, dst, send_sem, recv_sem, target):
        return pltpu.make_async_remote_copy(
            src_ref=src, dst_ref=dst, send_sem=send_sem, recv_sem=recv_sem,
            device_id=target, device_id_type=MESH,
        )

    def across(phase, src, dst):
        copies = []
        for step in ORDER:
            other = lax.rem(y + step, ROW)
            copy = remote(
                src.at[other], dst.at[y], a_send.at[phase, step], a_recv.at[phase, y],
                (z * ROW + other, head),
            )
            copy.start()
            copies.append(copy)
        dst[pl.ds(y, 1)] = src[pl.ds(y, 1)]
        return copies

    def arrive(phase, dst):
        for step in range(1, ROW):
            other = lax.rem(y + step, ROW)
            remote(
                dst.at[other], dst.at[other], a_send.at[phase, step], a_recv.at[phase, other],
                (z * ROW + other, head),
            ).wait_recv()

    def factor_of(tile):
        row = jnp.where(odd == 1, tile[32:33], tile[36:37])
        return jnp.broadcast_to(row, (PART, TOK))

    def join(near, far):
        return jnp.where(data, near, 0.0) + factor_of(near) * far

    def row_scan(base, forward, arrived, prefix, zo, zi, result, returned):
        arrive(base, arrived)
        order = range(ROW) if forward else range(ROW - 1, -1, -1)
        running = jnp.where(data, 0.0, 1.0)
        for place in order:
            prefix[place] = running
            running = join(arrived[place], running)
        zo[0] = running
        sign = 1 if forward else -1
        sends = []
        for n, (slot, step) in enumerate(((0, sign), (0, 2 * sign))):
            copy = remote(
                zo.at[slot], zi.at[n], z_send.at[base, n], z_recv.at[base, n], (at_row(step), head)
            )
            copy.start()
            sends.append(copy)
        sends[0].wait_recv()
        sends[1].wait_recv()
        pair = join(zi[0], zi[1])
        zo[1] = pair
        copy = remote(
            zo.at[1], zi.at[2], z_send.at[base, 2], z_recv.at[base, 2], (at_row(2 * sign), head)
        )
        copy.start()
        sends.append(copy)
        copy.wait_recv()
        entry = pair + factor_of(pair) * zi[2]
        for step in ORDER:
            other = lax.rem(y + step, ROW)
            tile = prefix[other]
            result[pl.ds(other, 1)] = (tile + factor_of(tile) * entry)[None]
            copy = remote(
                result.at[other], returned.at[y], a_send.at[base + 1, step],
                a_recv.at[base + 1, y], (z * ROW + other, head),
            )
            copy.start()
            sends.append(copy)
        tile = prefix[y]
        returned[pl.ds(y, 1)] = (tile + factor_of(tile) * entry)[None]
        arrive(base + 1, returned)
        return sends

    pending = across(0, up, up_in)

    loads[4].wait()
    loads[5].wait()
    q_heads = heads_of(q_ref)
    g_heads = heads_of(g_ref)
    for h in range(HEADS):
        row = sums[h : h + 1, :]
        final = row[:, TOK - 1 : TOK]
        col = spread(row)
        qb = q_heads[h].astype(BF16)
        qh[h] = qb
        gh[h] = g_heads[h].astype(BF16)
        qt[h] = jnp.transpose(q_heads[h]) * (jnp.exp(row) * enter_row * FACTOR)
        ent[h] = jnp.exp(col) * enter_col * FACTOR
        leave[h] = jnp.exp(final - col) * leave_col
        weight = jnp.where(inside, jnp.exp(jnp.minimum(col - row, 0.0)), 0.0)
        within[h] = weight
        scores = weight * (nt(qb, kh[h]) * FACTOR)
        score[h] = scores
        out[h] = two(nn, split(scores), vh[h])

    pending += row_scan(0, True, up_in, part, zout, zin, back, back_in)

    squares = jnp.zeros((TOK, TOK), F32)
    dots = jnp.zeros((TOK, TOK), F32)
    for h in range(HEADS):
        pair = split(unpack(back_in, h))
        state_hi[h] = pair[0]
        state_lo[h] = pair[1]
        now = out[h] + ent[h] * two_right(nn, qh[h], pair)
        out[h] = now
        squares = squares + now * now
        dots = dots + now * gh[h].astype(F32)
    square_row = jnp.sum(jnp.transpose(squares), axis=0, keepdims=True)
    dot_row = jnp.sum(jnp.transpose(dots), axis=0, keepdims=True)
    small = lax.broadcasted_iota(jnp.int32, (8, TOK), 0)
    tile = jnp.where(small == 0, square_row, dot_row)
    hsend[...] = tile
    for step in range(1, HEAD_DEVS):
        other = lax.rem(head + step, HEAD_DEVS)
        copy = remote(hsend, hrecv.at[head], h_send.at[step], h_recv.at[head], (ctx, other))
        copy.start()
        pending.append(copy)
    hrecv[pl.ds(head, 1)] = tile[None]
    for h in range(HEADS):
        pair = split(out[h])
        out_hi[h] = pair[0]
        out_lo[h] = pair[1]
    for step in range(1, HEAD_DEVS):
        other = lax.rem(head + step, HEAD_DEVS)
        remote(
            hrecv.at[other], hrecv.at[other], h_send.at[step], h_recv.at[other], (ctx, other)
        ).wait_recv()
    total = hrecv[0]
    for slot in range(1, HEAD_DEVS):
        total = total + hrecv[slot]
    rscale = lax.rsqrt(total[0:1] / FULL + EPS)
    drift = rscale * rscale * rscale * total[1:2] / FULL

    for h in range(HEADS):
        near = split(qt[h] * rscale)
        far = split(qt[h] * drift)
        pulled = two(nn, near, gh[h]) - three(nn, far, (out_hi[h], out_lo[h]))
        pack(pulled, passing[h], 2 * h, upb)

    pending += across(2, upb, upb_in)

    rscale_col = spread(rscale)
    drift_col = spread(drift)
    normed = []
    grads = []
    for h in range(HEADS):
        now = out[h]
        normed.append(now * rscale_col)
        grad_pair = split(rscale_col * gh[h].astype(F32) - drift_col * now)
        mixed = within[h] * two(nt, grad_pair, vh[h])
        grads.append(
            FACTOR * two(nn, split(mixed), kh[h])
            + ent[h] * three(nt, grad_pair, (state_hi[h], state_lo[h]))
        )
        dkl[h] = FACTOR * two(nn, split(jnp.transpose(mixed)), qh[h])
        dvl[h] = three(nn, split(jnp.transpose(score[h])), grad_pair)
    put_heads(att_ref, normed)
    put_heads(dq_ref, grads)
    stores = [
        pltpu.make_async_copy(src, dst, out_sem.at[n])
        for n, (src, dst) in enumerate(
            ((att_ref, att_hbm), (dq_ref, dq_hbm), (dk_ref, dk_hbm), (dv_ref, dv_hbm))
        )
    ]
    stores[0].start()
    stores[1].start()

    pending += row_scan(2, False, upb_in, partb, zoutb, zinb, backb, backb_in)

    state_pairs = [split(unpack(backb_in, h)) for h in range(HEADS)]
    put_heads(
        dk_ref, [dkl[h] + leave[h] * two_right(nt, vh[h], state_pairs[h]) for h in range(HEADS)]
    )
    stores[2].start()
    put_heads(
        dv_ref, [dvl[h] + leave[h] * two_right(nn, kh[h], state_pairs[h]) for h in range(HEADS)]
    )
    stores[3].start()
    for copy in pending:
        copy.wait_send()
    for store in stores:
        store.wait()


def write(*refs):
    srcs, dsts, sem = refs[0:4], refs[4:8], refs[8]
    copies = [pltpu.make_async_copy(a, b, sem.at[n]) for n, (a, b) in enumerate(zip(srcs, dsts))]
    for copy in copies:
        copy.start()
    for copy in copies:
        copy.wait()


def local(queries, key_vectors, value_vectors, out_grad, log_decay, doc_ids):
    square_bf = pltpu.VMEM((HEADS, TOK, TOK), BF16)
    square_f = pltpu.VMEM((HEADS, TOK, TOK), F32)
    slices = pltpu.VMEM((ROW, PART, TOK), F32)
    scan = [slices] * 5 + [pltpu.VMEM((2, PART, TOK), F32), pltpu.VMEM((3, PART, TOK), F32)]
    dma = pltpu.SemaphoreType.DMA
    result = jax.ShapeDtypeStruct((TOK, WIDTH), BF16)
    hbm = pl.BlockSpec(memory_space=pltpu.HBM)
    results = pl.pallas_call(
        kernel,
        out_shape=[result] * 4,
        in_specs=[hbm] * 6,
        out_specs=[hbm] * 4,
        scratch_shapes=[pltpu.VMEM((TOK, WIDTH), BF16)] * 4 + [dma((4,))]
        + [pltpu.VMEM((TOK, WIDTH), BF16)] * 4
        + [pltpu.VMEM((HEADS, TOK), F32), pltpu.VMEM((ROW * ROWS, TOK), jnp.int32), dma((6,))]
        + [square_bf] * 4
        + [square_f] * 6
        + [square_bf] * 4
        + [square_f] * 2
        + scan * 2
        + [pltpu.VMEM((8, TOK), F32), pltpu.VMEM((HEAD_DEVS, 8, TOK), F32)]
        + [dma((4, ROW)), dma((4, ROW)), dma((4, 3)), dma((4, 3)), dma((8,)), dma((8,))],
        compiler_params=pltpu.CompilerParams(
            collective_id=0, has_side_effects=True, vmem_limit_bytes=60 << 20
        ),
    )(
        queries, key_vectors, value_vectors, out_grad, log_decay,
        doc_ids.reshape(ROW * ROWS, TOK),
    )
    return pl.pallas_call(
        write,
        out_shape=[result] * 4,
        in_specs=[pl.BlockSpec(memory_space=pltpu.VMEM)] * 4,
        out_specs=[hbm] * 4,
        scratch_shapes=[dma((4,))],
    )(*results)


def solution(mesh):
    return jax.shard_map(
        local,
        mesh=mesh,
        in_specs=(
            P("ctx", "head"), P("ctx", "head"), P("ctx", "head"), P("ctx", "head"),
            P("head", "ctx"), P(),
        ),
        out_specs=(P("ctx", "head"),) * 4,
        check_vma=False,
    )
```

```python
import jax
import jax.numpy as jnp
from jax import lax
from jax.experimental import pallas as pl
from jax.experimental.pallas import tpu as pltpu
from jax.sharding import PartitionSpec as P

HEADS = 4
DH = 96
TOK = 128
WIDTH = HEADS * DH
FULL = 3072
ROW = 8
ROWS = 12
HEAD_DEVS = 8
PART = 40
ORDER = (4, 3, 5, 2, 6, 1, 7)
EPS = 1e-05
FACTOR = DH ** (-0.5)
F32 = jnp.float32
BF16 = jnp.bfloat16
MESH = pl.DeviceIdType.MESH


def nn(a, b):
    return lax.dot_general(a, b, (((1,), (0,)), ((), ())), preferred_element_type=F32)


def nt(a, b):
    return lax.dot_general(a, b, (((1,), (1,)), ((), ())), preferred_element_type=F32)


def split(x):
    hi = x.astype(BF16)
    return hi, (x - hi.astype(F32)).astype(BF16)


def two(dot, a, b):
    return dot(a[0], b) + dot(a[1], b)


def two_right(dot, a, b):
    return dot(a, b[0]) + dot(a, b[1])


def three(dot, a, b):
    return dot(a[0], b[0]) + (dot(a[0], b[1]) + dot(a[1], b[0]))


def kernel(
    q_hbm, k_hbm, v_hbm, g_hbm, ld_hbm, doc_hbm,
    att_hbm, dq_hbm, dk_hbm, dv_hbm,
    att_ref, dq_ref, dk_ref, dv_ref, out_sem,
    q_ref, k_ref, v_ref, g_ref, ld_ref, doc_ref, in_sem,
    qh, kh, vh, gh, qt, within, score, ent, leave, out, state_hi, state_lo,
    out_hi, out_lo, dkl, dvl,
    up, up_in, part, back, back_in, zout, zin,
    upb, upb_in, partb, backb, backb_in, zoutb, zinb,
    hsend, hrecv,
    a_send, a_recv, z_send, z_recv, h_send, h_recv,
):
    ctx = lax.axis_index("ctx")
    head = lax.axis_index("head")
    y = lax.rem(ctx, ROW)
    z = ctx // ROW

    def at_row(step):
        return lax.rem(z + step + ROWS, ROWS) * ROW + y

    barrier = pltpu.get_barrier_semaphore()
    for step in range(1, ROW):
        pl.semaphore_signal(
            barrier, inc=1, device_id=(z * ROW + lax.rem(y + step, ROW), head), device_id_type=MESH
        )
    for step in (-2, -1, 1, 2):

        @pl.when((z + step >= 0) & (z + step < ROWS))
        def _(step=step):
            pl.semaphore_signal(barrier, inc=1, device_id=(at_row(step), head), device_id_type=MESH)

    for step in range(1, HEAD_DEVS):
        pl.semaphore_signal(
            barrier, inc=1, device_id=(ctx, lax.rem(head + step, HEAD_DEVS)), device_id_type=MESH
        )

    loads = [
        pltpu.make_async_copy(src, dst, in_sem.at[n])
        for n, (src, dst) in enumerate((
            (ld_hbm, ld_ref), (doc_hbm, doc_ref), (k_hbm, k_ref),
            (v_hbm, v_ref), (q_hbm, q_ref), (g_hbm, g_ref),
        ))
    ]
    for load in loads:
        load.start()

    lane = lax.broadcasted_iota(jnp.int32, (TOK, TOK), 1)
    sub = lax.broadcasted_iota(jnp.int32, (TOK, TOK), 0)
    real = lane < DH
    odd = lax.rem(y, 2)
    part_sub = lax.broadcasted_iota(jnp.int32, (PART, TOK), 0)
    data = (part_sub < 32) | (part_sub // 4 == 8 + odd)
    wide = lax.broadcasted_iota(jnp.int32, (72, TOK), 1) < DH
    third = lax.broadcasted_iota(jnp.int32, (24, TOK), 1)
    low = lax.broadcasted_iota(jnp.int32, (8, TOK), 0) < 4

    def heads_of(ref):
        tiles = [ref[:, TOK * t : TOK * t + TOK].astype(F32) for t in range(3)]
        zero = jnp.zeros((TOK, TOK), F32)
        h0 = tiles[0]
        h1 = pltpu.roll(jnp.where(lane >= 96, tiles[0], tiles[1]), 32, 1)
        h2 = pltpu.roll(jnp.where(lane >= 64, tiles[1], tiles[2]), 64, 1)
        h3 = pltpu.roll(tiles[2], 96, 1)
        return [jnp.where(real, h, zero) for h in (h0, h1, h2, h3)]

    def put_heads(ref, parts):
        r1 = pltpu.roll(parts[1], 96, 1)
        r2 = pltpu.roll(parts[2], 64, 1)
        r3 = pltpu.roll(parts[3], 32, 1)
        ref[:, 0:TOK] = jnp.where(lane < 96, parts[0], r1).astype(BF16)
        ref[:, TOK : 2 * TOK] = jnp.where(lane < 64, r1, r2).astype(BF16)
        ref[:, 2 * TOK : 3 * TOK] = jnp.where(lane < 32, r2, r3).astype(BF16)

    def spread(row):
        return jnp.transpose(jnp.broadcast_to(row, (TOK, TOK)))

    loads[0].wait()
    loads[1].wait()
    upper = (sub <= lane).astype(F32)
    sums = lax.dot_general(
        ld_ref[...], upper, (((1,), (0,)), ((), ())),
        precision=lax.Precision.HIGHEST, preferred_element_type=F32,
    )
    doc_row = doc_ref[pl.ds(ctx, 1), :].astype(F32)
    earlier = doc_ref[pl.ds(jnp.maximum(ctx - 1, 0), 1), :].astype(F32)[:, TOK - 1 : TOK]
    before = jnp.where(ctx > 0, earlier, -1.0)
    last = doc_row[:, TOK - 1 : TOK]
    enter_row = (doc_row == before).astype(F32)
    leave_row = (doc_row == last).astype(F32)
    through = (last == before).astype(F32)
    doc_col = spread(doc_row)
    inside = (sub >= lane) & (doc_col == doc_row)
    enter_col = (doc_col == before).astype(F32)
    leave_col = (doc_col == last).astype(F32)

    def pack(state, decay, slot, dest):
        tail = state[72:96]
        rest = jnp.concatenate(
            [pltpu.roll(tail, 96, 1), pltpu.roll(tail, 64, 1), pltpu.roll(tail, 32, 1)], axis=0
        )
        full = jnp.where(wide, state[0:72], rest)
        dest[slot, 0:32] = full[0:32]
        dest[slot, 32:40] = jnp.where(low, full[32:40], decay)
        dest[slot + 1, 0:32] = full[40:72]
        dest[slot + 1, 32:40] = jnp.where(low, decay, full[32:40])

    def unpack(arrived, h):
        one, other = arrived[2 * h], arrived[2 * h + 1]
        full = jnp.concatenate(
            [one[0:32], jnp.where(low, one[32:40], other[32:40]), other[0:32]], axis=0
        )
        tail = jnp.where(
            third < 32, pltpu.roll(full[0:24], 32, 1),
            jnp.where(third < 64, pltpu.roll(full[24:48], 64, 1), pltpu.roll(full[48:72], 96, 1)),
        )
        tail = jnp.where(third < DH, tail, 0.0)
        return jnp.concatenate(
            [jnp.where(wide, full, 0.0), tail, jnp.zeros((TOK - DH, TOK), F32)], axis=0
        )

    loads[2].wait()
    loads[3].wait()
    k_heads = heads_of(k_ref)
    v_heads = heads_of(v_ref)
    passing = []
    for h in range(HEADS):
        row = sums[h : h + 1, :]
        final = row[:, TOK - 1 : TOK]
        passing.append(jnp.exp(final) * through)
        vb = v_heads[h].astype(BF16)
        vh[h] = vb
        kh[h] = k_heads[h].astype(BF16)
        kt = jnp.transpose(k_heads[h]) * (jnp.exp(final - row) * leave_row)
        update = two(nn, split(kt), vb)
        pack(update, passing[h], 2 * h, up)

    rows_near = jnp.minimum(z, 2) + jnp.minimum(ROWS - 1 - z, 2)
    pl.semaphore_wait(barrier, (ROW - 1) + (HEAD_DEVS - 1) + rows_near)

    def remote(src, dst, send_sem, recv_sem, target):
        return pltpu.make_async_remote_copy(
            src_ref=src, dst_ref=dst, send_sem=send_sem, recv_sem=recv_sem,
            device_id=target, device_id_type=MESH,
        )

    def across(phase, src, dst):
        copies = []
        for step in ORDER:
            other = lax.rem(y + step, ROW)
            copy = remote(
                src.at[other], dst.at[y], a_send.at[phase, step], a_recv.at[phase, y],
                (z * ROW + other, head),
            )
            copy.start()
            copies.append((None, copy))
        dst[pl.ds(y, 1)] = src[pl.ds(y, 1)]
        return copies

    def arrive(phase, dst):
        for step in range(1, ROW):
            other = lax.rem(y + step, ROW)
            remote(
                dst.at[other], dst.at[other], a_send.at[phase, step], a_recv.at[phase, other],
                (z * ROW + other, head),
            ).wait_recv()

    def factor_of(tile):
        row = jnp.where(odd == 1, tile[32:33], tile[36:37])
        return jnp.broadcast_to(row, (PART, TOK))

    def join(near, far):
        return jnp.where(data, near, 0.0) + factor_of(near) * far

    def row_scan(base, forward, arrived, prefix, zo, zi, result, returned):
        arrive(base, arrived)
        order = range(ROW) if forward else range(ROW - 1, -1, -1)
        running = jnp.where(data, 0.0, 1.0)
        for place in order:
            prefix[place] = running
            running = join(arrived[place], running)
        zo[0] = running
        sign = 1 if forward else -1
        place_z = z if forward else ROWS - 1 - z
        for n in range(3):

            @pl.when(place_z <= n)
            def _(n=n):
                zi[n] = jnp.zeros((PART, TOK), F32)

        def hop(n):
            distance = 1 if n == 0 else 2
            return remote(
                zo.at[n // 2], zi.at[n], z_send.at[base, n], z_recv.at[base, n],
                (at_row(sign * distance), head),
            )

        sending = (place_z < ROWS - 1, place_z < ROWS - 2, (place_z > 0) & (place_z < ROWS - 2))
        sends = []

        def send_hop(n):
            copy = hop(n)

            @pl.when(sending[n])
            def _():
                copy.start()

            sends.append((sending[n], copy))

        def get_hop(n):
            @pl.when(place_z > n)
            def _():
                hop(n).wait_recv()

        send_hop(1)
        send_hop(0)
        get_hop(0)
        get_hop(1)
        pair = join(zi[0], zi[1])
        zo[1] = pair
        send_hop(2)
        get_hop(2)
        entry = pair + factor_of(pair) * zi[2]
        for step in ORDER:
            other = lax.rem(y + step, ROW)
            tile = prefix[other]
            result[pl.ds(other, 1)] = (tile + factor_of(tile) * entry)[None]
            copy = remote(
                result.at[other], returned.at[y], a_send.at[base + 1, step],
                a_recv.at[base + 1, y], (z * ROW + other, head),
            )
            copy.start()
            sends.append((None, copy))
        tile = prefix[y]
        returned[pl.ds(y, 1)] = (tile + factor_of(tile) * entry)[None]
        arrive(base + 1, returned)
        return sends

    pending = across(0, up, up_in)

    loads[4].wait()
    loads[5].wait()
    q_heads = heads_of(q_ref)
    g_heads = heads_of(g_ref)
    for h in range(HEADS):
        row = sums[h : h + 1, :]
        final = row[:, TOK - 1 : TOK]
        col = spread(row)
        qb = q_heads[h].astype(BF16)
        qh[h] = qb
        gh[h] = g_heads[h].astype(BF16)
        qt[h] = jnp.transpose(q_heads[h]) * (jnp.exp(row) * enter_row * FACTOR)
        ent[h] = jnp.exp(col) * enter_col * FACTOR
        leave[h] = jnp.exp(final - col) * leave_col
        weight = jnp.where(inside, jnp.exp(jnp.minimum(col - row, 0.0)), 0.0)
        within[h] = weight
        scores = weight * (nt(qb, kh[h]) * FACTOR)
        score[h] = scores
        out[h] = two(nn, split(scores), vh[h])

    pending += row_scan(0, True, up_in, part, zout, zin, back, back_in)

    squares = jnp.zeros((TOK, TOK), F32)
    dots = jnp.zeros((TOK, TOK), F32)
    for h in range(HEADS):
        pair = split(unpack(back_in, h))
        state_hi[h] = pair[0]
        state_lo[h] = pair[1]
        now = out[h] + ent[h] * two_right(nn, qh[h], pair)
        out[h] = now
        squares = squares + now * now
        dots = dots + now * gh[h].astype(F32)
    square_row = jnp.sum(jnp.transpose(squares), axis=0, keepdims=True)
    dot_row = jnp.sum(jnp.transpose(dots), axis=0, keepdims=True)
    small = lax.broadcasted_iota(jnp.int32, (8, TOK), 0)
    tile = jnp.where(small == 0, square_row, dot_row)
    hsend[...] = tile
    for step in range(1, HEAD_DEVS):
        other = lax.rem(head + step, HEAD_DEVS)
        copy = remote(hsend, hrecv.at[head], h_send.at[step], h_recv.at[head], (ctx, other))
        copy.start()
        pending.append((None, copy))
    hrecv[pl.ds(head, 1)] = tile[None]
    for h in range(HEADS):
        pair = split(out[h])
        out_hi[h] = pair[0]
        out_lo[h] = pair[1]
    for step in range(1, HEAD_DEVS):
        other = lax.rem(head + step, HEAD_DEVS)
        remote(
            hrecv.at[other], hrecv.at[other], h_send.at[step], h_recv.at[other], (ctx, other)
        ).wait_recv()
    total = hrecv[0]
    for slot in range(1, HEAD_DEVS):
        total = total + hrecv[slot]
    rscale = lax.rsqrt(total[0:1] / FULL + EPS)
    drift = rscale * rscale * rscale * total[1:2] / FULL

    for h in range(HEADS):
        near = split(qt[h] * rscale)
        far = split(qt[h] * drift)
        pulled = two(nn, near, gh[h]) - three(nn, far, (out_hi[h], out_lo[h]))
        pack(pulled, passing[h], 2 * h, upb)

    pending += across(2, upb, upb_in)

    rscale_col = spread(rscale)
    drift_col = spread(drift)
    normed = []
    grads = []
    for h in range(HEADS):
        now = out[h]
        normed.append(now * rscale_col)
        grad_pair = split(rscale_col * gh[h].astype(F32) - drift_col * now)
        mixed = within[h] * two(nt, grad_pair, vh[h])
        grads.append(
            FACTOR * two(nn, split(mixed), kh[h])
            + ent[h] * three(nt, grad_pair, (state_hi[h], state_lo[h]))
        )
        dkl[h] = FACTOR * two(nn, split(jnp.transpose(mixed)), qh[h])
        dvl[h] = three(nn, split(jnp.transpose(score[h])), grad_pair)
    put_heads(att_ref, normed)
    put_heads(dq_ref, grads)
    stores = [
        pltpu.make_async_copy(src, dst, out_sem.at[n])
        for n, (src, dst) in enumerate(
            ((att_ref, att_hbm), (dq_ref, dq_hbm), (dk_ref, dk_hbm), (dv_ref, dv_hbm))
        )
    ]
    stores[0].start()
    stores[1].start()

    pending += row_scan(2, False, upb_in, partb, zoutb, zinb, backb, backb_in)

    state_pairs = [split(unpack(backb_in, h)) for h in range(HEADS)]
    put_heads(
        dk_ref, [dkl[h] + leave[h] * two_right(nt, vh[h], state_pairs[h]) for h in range(HEADS)]
    )
    stores[2].start()
    put_heads(
        dv_ref, [dvl[h] + leave[h] * two_right(nn, kh[h], state_pairs[h]) for h in range(HEADS)]
    )
    stores[3].start()
    for condition, copy in pending:
        if condition is None:
            copy.wait_send()
        else:
            pl.when(condition)(copy.wait_send)
    for store in stores:
        store.wait()


def write(*refs):
    srcs, dsts, sem = refs[0:4], refs[4:8], refs[8]
    copies = [pltpu.make_async_copy(a, b, sem.at[n]) for n, (a, b) in enumerate(zip(srcs, dsts))]
    for copy in copies:
        copy.start()
    for copy in copies:
        copy.wait()


def local(queries, key_vectors, value_vectors, out_grad, log_decay, doc_ids):
    square_bf = pltpu.VMEM((HEADS, TOK, TOK), BF16)
    square_f = pltpu.VMEM((HEADS, TOK, TOK), F32)
    slices = pltpu.VMEM((ROW, PART, TOK), F32)
    scan = [slices] * 5 + [pltpu.VMEM((2, PART, TOK), F32), pltpu.VMEM((3, PART, TOK), F32)]
    dma = pltpu.SemaphoreType.DMA
    result = jax.ShapeDtypeStruct((TOK, WIDTH), BF16)
    hbm = pl.BlockSpec(memory_space=pltpu.HBM)
    results = pl.pallas_call(
        kernel,
        out_shape=[result] * 4,
        in_specs=[hbm] * 6,
        out_specs=[hbm] * 4,
        scratch_shapes=[pltpu.VMEM((TOK, WIDTH), BF16)] * 4 + [dma((4,))]
        + [pltpu.VMEM((TOK, WIDTH), BF16)] * 4
        + [pltpu.VMEM((HEADS, TOK), F32), pltpu.VMEM((ROW * ROWS, TOK), jnp.int32), dma((6,))]
        + [square_bf] * 4
        + [square_f] * 6
        + [square_bf] * 4
        + [square_f] * 2
        + scan * 2
        + [pltpu.VMEM((8, TOK), F32), pltpu.VMEM((HEAD_DEVS, 8, TOK), F32)]
        + [dma((4, ROW)), dma((4, ROW)), dma((4, 3)), dma((4, 3)), dma((8,)), dma((8,))],
        compiler_params=pltpu.CompilerParams(
            collective_id=0, has_side_effects=True, vmem_limit_bytes=60 << 20
        ),
    )(
        queries, key_vectors, value_vectors, out_grad, log_decay,
        doc_ids.reshape(ROW * ROWS, TOK),
    )
    return pl.pallas_call(
        write,
        out_shape=[result] * 4,
        in_specs=[pl.BlockSpec(memory_space=pltpu.VMEM)] * 4,
        out_specs=[hbm] * 4,
        scratch_shapes=[dma((4,))],
    )(*results)


def solution(mesh):
    return jax.shard_map(
        local,
        mesh=mesh,
        in_specs=(
            P("ctx", "head"), P("ctx", "head"), P("ctx", "head"), P("ctx", "head"),
            P("head", "ctx"), P(),
        ),
        out_specs=(P("ctx", "head"),) * 4,
        check_vma=False,
    )
```

```python
import jax
import jax.numpy as jnp
from jax import lax
from jax.experimental import pallas as pl
from jax.experimental.pallas import tpu as pltpu
from jax.sharding import PartitionSpec as P

HEADS = 4
DH = 96
TOK = 128
WIDTH = HEADS * DH
FULL = 3072
ROW = 8
ROWS = 12
HEAD_DEVS = 8
PART = 40
USED = 36
ORDER = (4, 3, 5, 2, 6, 1, 7)
EPS = 1e-05
FACTOR = DH ** (-0.5)
F32 = jnp.float32
BF16 = jnp.bfloat16
MESH = pl.DeviceIdType.MESH


def nn(a, b):
    return lax.dot_general(a, b, (((1,), (0,)), ((), ())), preferred_element_type=F32)


def nt(a, b):
    return lax.dot_general(a, b, (((1,), (1,)), ((), ())), preferred_element_type=F32)


def split(x):
    hi = x.astype(BF16)
    return hi, (x - hi.astype(F32)).astype(BF16)


def two(dot, a, b):
    return dot(a[0], b) + dot(a[1], b)


def two_right(dot, a, b):
    return dot(a, b[0]) + dot(a, b[1])


def three(dot, a, b):
    return dot(a[0], b[0]) + (dot(a[0], b[1]) + dot(a[1], b[0]))


def kernel(
    q_hbm, k_hbm, v_hbm, g_hbm, ld_hbm, doc_hbm,
    att_ref, dq_ref, dk_ref, dv_ref,
    q_ref, k_ref, v_ref, g_ref, ld_ref, doc_ref, in_sem,
    qh, kh, vh, gh, qt, within, score, ent, leave, out, state_hi, state_lo,
    out_hi, out_lo, dkl, dvl,
    up, up_in, part, back, back_in, zout, zin,
    upb, upb_in, partb, backb, backb_in, zoutb, zinb,
    hsend, hrecv,
    a_send, a_recv, z_send, z_recv, h_send, h_recv,
):
    ctx = lax.axis_index("ctx")
    head = lax.axis_index("head")
    y = lax.rem(ctx, ROW)
    z = ctx // ROW

    def at_row(step):
        return lax.rem(z + step + ROWS, ROWS) * ROW + y

    barrier = pltpu.get_barrier_semaphore()
    for step in range(1, ROW):
        pl.semaphore_signal(
            barrier, inc=1, device_id=(z * ROW + lax.rem(y + step, ROW), head), device_id_type=MESH
        )
    for step in (-2, -1, 1, 2):

        @pl.when((z + step >= 0) & (z + step < ROWS))
        def _(step=step):
            pl.semaphore_signal(barrier, inc=1, device_id=(at_row(step), head), device_id_type=MESH)

    for step in range(1, HEAD_DEVS):
        pl.semaphore_signal(
            barrier, inc=1, device_id=(ctx, lax.rem(head + step, HEAD_DEVS)), device_id_type=MESH
        )

    loads = [
        pltpu.make_async_copy(src, dst, in_sem.at[n])
        for n, (src, dst) in enumerate((
            (ld_hbm, ld_ref), (doc_hbm, doc_ref), (k_hbm, k_ref),
            (v_hbm, v_ref), (q_hbm, q_ref), (g_hbm, g_ref),
        ))
    ]
    for load in loads:
        load.start()

    lane = lax.broadcasted_iota(jnp.int32, (TOK, TOK), 1)
    sub = lax.broadcasted_iota(jnp.int32, (TOK, TOK), 0)
    real = lane < DH
    part_sub = lax.broadcasted_iota(jnp.int32, (PART, TOK), 0)
    data = part_sub < USED
    wide = lax.broadcasted_iota(jnp.int32, (72, TOK), 1) < DH
    third = lax.broadcasted_iota(jnp.int32, (24, TOK), 1)
    low = lax.broadcasted_iota(jnp.int32, (8, TOK), 0) < 4

    def heads_of(ref):
        tiles = [ref[:, TOK * t : TOK * t + TOK].astype(F32) for t in range(3)]
        zero = jnp.zeros((TOK, TOK), F32)
        h0 = tiles[0]
        h1 = pltpu.roll(jnp.where(lane >= 96, tiles[0], tiles[1]), 32, 1)
        h2 = pltpu.roll(jnp.where(lane >= 64, tiles[1], tiles[2]), 64, 1)
        h3 = pltpu.roll(tiles[2], 96, 1)
        return [jnp.where(real, h, zero) for h in (h0, h1, h2, h3)]

    def put_heads(ref, parts):
        r1 = pltpu.roll(parts[1], 96, 1)
        r2 = pltpu.roll(parts[2], 64, 1)
        r3 = pltpu.roll(parts[3], 32, 1)
        ref[:, 0:TOK] = jnp.where(lane < 96, parts[0], r1).astype(BF16)
        ref[:, TOK : 2 * TOK] = jnp.where(lane < 64, r1, r2).astype(BF16)
        ref[:, 2 * TOK : 3 * TOK] = jnp.where(lane < 32, r2, r3).astype(BF16)

    def spread(row):
        return jnp.transpose(jnp.broadcast_to(row, (TOK, TOK)))

    loads[0].wait()
    loads[1].wait()
    upper = (sub <= lane).astype(F32)
    sums = lax.dot_general(
        ld_ref[...], upper, (((1,), (0,)), ((), ())),
        precision=lax.Precision.HIGHEST, preferred_element_type=F32,
    )
    doc_row = doc_ref[pl.ds(ctx, 1), :].astype(F32)
    earlier = doc_ref[pl.ds(jnp.maximum(ctx - 1, 0), 1), :].astype(F32)[:, TOK - 1 : TOK]
    before = jnp.where(ctx > 0, earlier, -1.0)
    last = doc_row[:, TOK - 1 : TOK]
    enter_row = (doc_row == before).astype(F32)
    leave_row = (doc_row == last).astype(F32)
    through = (last == before).astype(F32)
    doc_col = spread(doc_row)
    inside = (sub >= lane) & (doc_col == doc_row)
    enter_col = (doc_col == before).astype(F32)
    leave_col = (doc_col == last).astype(F32)

    def pack(state, decay, slot, dest):
        tail = state[72:96]
        rest = jnp.concatenate(
            [pltpu.roll(tail, 96, 1), pltpu.roll(tail, 64, 1), pltpu.roll(tail, 32, 1)], axis=0
        )
        full = jnp.where(wide, state[0:72], rest)
        dest[slot, 0:32] = full[0:32]
        dest[slot, 32:40] = jnp.where(low, full[32:40], decay)
        dest[slot + 1, 0:32] = full[40:72]
        dest[slot + 1, 32:40] = jnp.where(low, pltpu.roll(full[32:40], 4, 0), decay)

    def unpack(arrived, h):
        one, other = arrived[2 * h], arrived[2 * h + 1]
        full = jnp.concatenate(
            [one[0:32], jnp.where(low, one[32:40], pltpu.roll(other[32:40], 4, 0)), other[0:32]], axis=0
        )
        tail = jnp.where(
            third < 32, pltpu.roll(full[0:24], 32, 1),
            jnp.where(third < 64, pltpu.roll(full[24:48], 64, 1), pltpu.roll(full[48:72], 96, 1)),
        )
        tail = jnp.where(third < DH, tail, 0.0)
        return jnp.concatenate(
            [jnp.where(wide, full, 0.0), tail, jnp.zeros((TOK - DH, TOK), F32)], axis=0
        )

    loads[2].wait()
    loads[3].wait()
    k_heads = heads_of(k_ref)
    v_heads = heads_of(v_ref)
    passing = []
    for h in range(HEADS):
        row = sums[h : h + 1, :]
        final = row[:, TOK - 1 : TOK]
        passing.append(jnp.exp(final) * through)
        vb = v_heads[h].astype(BF16)
        vh[h] = vb
        kh[h] = k_heads[h].astype(BF16)
        kt = jnp.transpose(k_heads[h]) * (jnp.exp(final - row) * leave_row)
        update = two(nn, split(kt), vb)
        pack(update, passing[h], 2 * h, up)

    rows_near = jnp.minimum(z, 2) + jnp.minimum(ROWS - 1 - z, 2)
    pl.semaphore_wait(barrier, (ROW - 1) + (HEAD_DEVS - 1) + rows_near)

    def remote(src, dst, send_sem, recv_sem, target):
        return pltpu.make_async_remote_copy(
            src_ref=src, dst_ref=dst, send_sem=send_sem, recv_sem=recv_sem,
            device_id=target, device_id_type=MESH,
        )

    def across(phase, src, dst, rows):
        copies = []
        for step in ORDER:
            other = lax.rem(y + step, ROW)
            copy = remote(
                src.at[other, pl.ds(0, rows)], dst.at[y, pl.ds(0, rows)],
                a_send.at[phase, step], a_recv.at[phase, y],
                (z * ROW + other, head),
            )
            copy.start()
            copies.append((None, copy))
        dst[pl.ds(y, 1)] = src[pl.ds(y, 1)]
        return copies

    def arrive(phase, dst, rows):
        for step in range(1, ROW):
            other = lax.rem(y + step, ROW)
            remote(
                dst.at[other, pl.ds(0, rows)], dst.at[other, pl.ds(0, rows)],
                a_send.at[phase, step], a_recv.at[phase, other],
                (z * ROW + other, head),
            ).wait_recv()

    def factor_of(tile):
        return jnp.broadcast_to(tile[USED : USED + 1], (PART, TOK))

    def join(near, far, factor):
        return jnp.where(data, near, 0.0) + factor * far

    def row_scan(base, forward, arrived, prefix, zo, zi, result, returned):
        arrive(base, arrived, USED + 1 if forward else USED)
        order = range(ROW) if forward else range(ROW - 1, -1, -1)
        running = jnp.where(data, 0.0, 1.0)
        for place in order:
            prefix[place] = running
            running = join(arrived[place], running, factor_of(up_in[place]))
        zo[0] = running
        sign = 1 if forward else -1
        place_z = z if forward else ROWS - 1 - z
        for n in range(3):

            @pl.when(place_z <= n)
            def _(n=n):
                zi[n] = jnp.zeros((PART, TOK), F32)

        def hop(n):
            distance = 1 if n == 0 else 2
            return remote(
                zo.at[n // 2, pl.ds(0, USED + 1)], zi.at[n, pl.ds(0, USED + 1)], z_send.at[base, n], z_recv.at[base, n],
                (at_row(sign * distance), head),
            )

        sending = (place_z < ROWS - 1, place_z < ROWS - 2, (place_z > 0) & (place_z < ROWS - 2))
        sends = []

        def send_hop(n):
            copy = hop(n)

            @pl.when(sending[n])
            def _():
                copy.start()

            sends.append((sending[n], copy))

        def get_hop(n):
            @pl.when(place_z > n)
            def _():
                hop(n).wait_recv()

        send_hop(1)
        send_hop(0)
        get_hop(0)
        get_hop(1)
        pair = join(zi[0], zi[1], factor_of(zi[0]))
        zo[1] = pair
        send_hop(2)
        get_hop(2)
        entry = pair + factor_of(pair) * zi[2]
        for step in ORDER:
            other = lax.rem(y + step, ROW)
            tile = prefix[other]
            result[pl.ds(other, 1)] = (tile + factor_of(tile) * entry)[None]
            copy = remote(
                result.at[other, pl.ds(0, USED)], returned.at[y, pl.ds(0, USED)],
                a_send.at[base + 1, step], a_recv.at[base + 1, y], (z * ROW + other, head),
            )
            copy.start()
            sends.append((None, copy))
        tile = prefix[y]
        returned[pl.ds(y, 1)] = (tile + factor_of(tile) * entry)[None]
        arrive(base + 1, returned, USED)
        return sends

    pending = across(0, up, up_in, USED + 1)

    loads[4].wait()
    loads[5].wait()
    q_heads = heads_of(q_ref)
    g_heads = heads_of(g_ref)
    for h in range(HEADS):
        row = sums[h : h + 1, :]
        final = row[:, TOK - 1 : TOK]
        col = spread(row)
        qb = q_heads[h].astype(BF16)
        qh[h] = qb
        gh[h] = g_heads[h].astype(BF16)
        qt[h] = jnp.transpose(q_heads[h]) * (jnp.exp(row) * enter_row * FACTOR)
        ent[h] = jnp.exp(col) * enter_col * FACTOR
        leave[h] = jnp.exp(final - col) * leave_col
        weight = jnp.where(inside, jnp.exp(jnp.minimum(col - row, 0.0)), 0.0)
        within[h] = weight
        scores = weight * (nt(qb, kh[h]) * FACTOR)
        score[h] = scores
        out[h] = two(nn, split(scores), vh[h])

    pending += row_scan(0, True, up_in, part, zout, zin, back, back_in)

    squares = jnp.zeros((TOK, TOK), F32)
    dots = jnp.zeros((TOK, TOK), F32)
    for h in range(HEADS):
        pair = split(unpack(back_in, h))
        state_hi[h] = pair[0]
        state_lo[h] = pair[1]
        now = out[h] + ent[h] * two_right(nn, qh[h], pair)
        out[h] = now
        squares = squares + now * now
        dots = dots + now * gh[h].astype(F32)
    square_row = jnp.sum(jnp.transpose(squares), axis=0, keepdims=True)
    dot_row = jnp.sum(jnp.transpose(dots), axis=0, keepdims=True)
    small = lax.broadcasted_iota(jnp.int32, (8, TOK), 0)
    tile = jnp.where(small == 0, square_row, dot_row)
    hsend[...] = tile
    for step in range(1, HEAD_DEVS):
        other = lax.rem(head + step, HEAD_DEVS)
        copy = remote(hsend.at[pl.ds(0, 2)], hrecv.at[head, pl.ds(0, 2)], h_send.at[step], h_recv.at[head], (ctx, other))
        copy.start()
        pending.append((None, copy))
    hrecv[pl.ds(head, 1)] = tile[None]
    for h in range(HEADS):
        pair = split(out[h])
        out_hi[h] = pair[0]
        out_lo[h] = pair[1]
    for step in range(1, HEAD_DEVS):
        other = lax.rem(head + step, HEAD_DEVS)
        remote(
            hrecv.at[other, pl.ds(0, 2)], hrecv.at[other, pl.ds(0, 2)], h_send.at[step], h_recv.at[other], (ctx, other)
        ).wait_recv()
    total = hrecv[0, 0:2]
    for slot in range(1, HEAD_DEVS):
        total = total + hrecv[slot, 0:2]
    rscale = lax.rsqrt(total[0:1] / FULL + EPS)
    drift = rscale * rscale * rscale * total[1:2] / FULL

    for h in range(HEADS):
        near = split(qt[h] * rscale)
        far = split(qt[h] * drift)
        pulled = two(nn, near, gh[h]) - three(nn, far, (out_hi[h], out_lo[h]))
        pack(pulled, passing[h], 2 * h, upb)

    pending += across(2, upb, upb_in, USED)

    rscale_col = spread(rscale)
    drift_col = spread(drift)
    normed = []
    grads = []
    for h in range(HEADS):
        now = out[h]
        normed.append(now * rscale_col)
        grad_pair = split(rscale_col * gh[h].astype(F32) - drift_col * now)
        mixed = within[h] * two(nt, grad_pair, vh[h])
        grads.append(
            FACTOR * two(nn, split(mixed), kh[h])
            + ent[h] * three(nt, grad_pair, (state_hi[h], state_lo[h]))
        )
        dkl[h] = FACTOR * two(nn, split(jnp.transpose(mixed)), qh[h])
        dvl[h] = three(nn, split(jnp.transpose(score[h])), grad_pair)
    put_heads(att_ref, normed)
    put_heads(dq_ref, grads)

    pending += row_scan(2, False, upb_in, partb, zoutb, zinb, backb, backb_in)

    state_pairs = [split(unpack(backb_in, h)) for h in range(HEADS)]
    put_heads(
        dk_ref, [dkl[h] + leave[h] * two_right(nt, vh[h], state_pairs[h]) for h in range(HEADS)]
    )
    put_heads(
        dv_ref, [dvl[h] + leave[h] * two_right(nn, kh[h], state_pairs[h]) for h in range(HEADS)]
    )
    for condition, copy in pending:
        if condition is None:
            copy.wait_send()
        else:
            pl.when(condition)(copy.wait_send)


def write(*refs):
    srcs, dsts, sem = refs[0:4], refs[4:8], refs[8]
    copies = [pltpu.make_async_copy(a, b, sem.at[n]) for n, (a, b) in enumerate(zip(srcs, dsts))]
    for copy in copies:
        copy.start()
    for copy in copies:
        copy.wait()


def local(queries, key_vectors, value_vectors, out_grad, log_decay, doc_ids):
    square_bf = pltpu.VMEM((HEADS, TOK, TOK), BF16)
    square_f = pltpu.VMEM((HEADS, TOK, TOK), F32)
    slices = pltpu.VMEM((ROW, PART, TOK), F32)
    scan = [slices] * 5 + [pltpu.VMEM((2, PART, TOK), F32), pltpu.VMEM((3, PART, TOK), F32)]
    dma = pltpu.SemaphoreType.DMA
    result = jax.ShapeDtypeStruct((TOK, WIDTH), BF16)
    vmem = pl.BlockSpec(memory_space=pltpu.VMEM)
    hbm = pl.BlockSpec(memory_space=pltpu.HBM)
    queries, key_vectors, value_vectors, out_grad, log_decay, docs = (
        pltpu.with_memory_space_constraint(x, pltpu.HBM)
        for x in (
            queries, key_vectors, value_vectors, out_grad, log_decay,
            doc_ids.reshape(ROW * ROWS, TOK),
        )
    )
    results = pl.pallas_call(
        kernel,
        out_shape=[result] * 4,
        in_specs=[hbm] * 6,
        out_specs=[vmem] * 4,
        scratch_shapes=[pltpu.VMEM((TOK, WIDTH), BF16)] * 4
        + [pltpu.VMEM((HEADS, TOK), F32), pltpu.VMEM((ROW * ROWS, TOK), jnp.int32), dma((6,))]
        + [square_bf] * 4
        + [square_f] * 6
        + [square_bf] * 4
        + [square_f] * 2
        + scan * 2
        + [pltpu.VMEM((8, TOK), F32), pltpu.VMEM((HEAD_DEVS, 8, TOK), F32)]
        + [dma((4, ROW)), dma((4, ROW)), dma((4, 3)), dma((4, 3)), dma((8,)), dma((8,))],
        compiler_params=pltpu.CompilerParams(
            collective_id=0, has_side_effects=True, vmem_limit_bytes=32 << 20
        ),
    )(
        queries, key_vectors, value_vectors, out_grad, log_decay, docs,
    )
    return pl.pallas_call(
        write,
        out_shape=[result] * 4,
        in_specs=[vmem] * 4,
        out_specs=[hbm] * 4,
        scratch_shapes=[dma((4,))],
    )(*(pltpu.with_memory_space_constraint(x, pltpu.VMEM) for x in results))


def solution(mesh):
    return jax.shard_map(
        local,
        mesh=mesh,
        in_specs=(
            P("ctx", "head"), P("ctx", "head"), P("ctx", "head"), P("ctx", "head"),
            P("head", "ctx"), P(),
        ),
        out_specs=(P("ctx", "head"),) * 4,
        check_vma=False,
    )
```

```python
import jax
import jax.numpy as jnp
from jax import lax
from jax.experimental import pallas as pl
from jax.experimental.pallas import tpu as pltpu
from jax.sharding import PartitionSpec as P

HEADS = 4
DH = 96
TOK = 128
WIDTH = HEADS * DH
FULL = 3072
ROW = 8
ROWS = 12
HEAD_DEVS = 8
PART = 40
USED = 36
ORDER = (4, 3, 5, 2, 6, 1, 7)
EPS = 1e-05
FACTOR = DH ** (-0.5)
F32 = jnp.float32
BF16 = jnp.bfloat16
MESH = pl.DeviceIdType.MESH


def nn(a, b):
    return lax.dot_general(a, b, (((1,), (0,)), ((), ())), preferred_element_type=F32)


def nt(a, b):
    return lax.dot_general(a, b, (((1,), (1,)), ((), ())), preferred_element_type=F32)


def split(x):
    hi = x.astype(BF16)
    return hi, (x - hi.astype(F32)).astype(BF16)


def two(dot, a, b):
    return dot(a[0], b) + dot(a[1], b)


def two_right(dot, a, b):
    return dot(a, b[0]) + dot(a, b[1])


def three(dot, a, b):
    return dot(a[0], b[0]) + (dot(a[0], b[1]) + dot(a[1], b[0]))


def kernel(
    q_hbm, k_hbm, v_hbm, g_hbm, ld_hbm, doc_hbm,
    att_ref, dq_ref, dk_ref, dv_ref,
    q_ref, k_ref, v_ref, g_ref, ld_ref, doc_ref, in_sem,
    qh, kh, vh, gh, qt, within, score, ent, leave, out, state_hi, state_lo,
    out_hi, out_lo, dkl, dvl,
    up, up_in, part, back, back_in, zout, zin,
    upb, upb_in, partb, backb, backb_in, zoutb, zinb,
    hsend, hrecv,
    a_send, a_recv, z_send, z_recv, h_send, h_recv,
):
    ctx = lax.axis_index("ctx")
    head = lax.axis_index("head")
    y = lax.rem(ctx, ROW)
    z = ctx // ROW

    def at_row(step):
        return lax.rem(z + step + ROWS, ROWS) * ROW + y

    barrier = pltpu.get_barrier_semaphore()
    for step in range(1, ROW):
        pl.semaphore_signal(
            barrier, inc=1, device_id=(z * ROW + lax.rem(y + step, ROW), head), device_id_type=MESH
        )
    for step in (-2, -1, 1, 2):

        @pl.when((z + step >= 0) & (z + step < ROWS))
        def _(step=step):
            pl.semaphore_signal(barrier, inc=1, device_id=(at_row(step), head), device_id_type=MESH)

    for step in range(1, HEAD_DEVS):
        pl.semaphore_signal(
            barrier, inc=1, device_id=(ctx, lax.rem(head + step, HEAD_DEVS)), device_id_type=MESH
        )

    loads = [
        pltpu.make_async_copy(src, dst, in_sem.at[n])
        for n, (src, dst) in enumerate((
            (ld_hbm, ld_ref), (doc_hbm, doc_ref), (k_hbm, k_ref),
            (v_hbm, v_ref), (q_hbm, q_ref), (g_hbm, g_ref),
        ))
    ]
    for load in loads:
        load.start()

    lane = lax.broadcasted_iota(jnp.int32, (TOK, TOK), 1)
    sub = lax.broadcasted_iota(jnp.int32, (TOK, TOK), 0)
    real = lane < DH
    part_sub = lax.broadcasted_iota(jnp.int32, (PART, TOK), 0)
    data = part_sub < USED
    wide = lax.broadcasted_iota(jnp.int32, (72, TOK), 1) < DH
    third = lax.broadcasted_iota(jnp.int32, (24, TOK), 1)
    low = lax.broadcasted_iota(jnp.int32, (8, TOK), 0) < 4

    def heads_of(ref):
        tiles = [ref[:, TOK * t : TOK * t + TOK].astype(F32) for t in range(3)]
        zero = jnp.zeros((TOK, TOK), F32)
        h0 = tiles[0]
        h1 = pltpu.roll(jnp.where(lane >= 96, tiles[0], tiles[1]), 32, 1)
        h2 = pltpu.roll(jnp.where(lane >= 64, tiles[1], tiles[2]), 64, 1)
        h3 = pltpu.roll(tiles[2], 96, 1)
        return [jnp.where(real, h, zero) for h in (h0, h1, h2, h3)]

    def put_heads(ref, parts):
        r1 = pltpu.roll(parts[1], 96, 1)
        r2 = pltpu.roll(parts[2], 64, 1)
        r3 = pltpu.roll(parts[3], 32, 1)
        ref[:, 0:TOK] = jnp.where(lane < 96, parts[0], r1).astype(BF16)
        ref[:, TOK : 2 * TOK] = jnp.where(lane < 64, r1, r2).astype(BF16)
        ref[:, 2 * TOK : 3 * TOK] = jnp.where(lane < 32, r2, r3).astype(BF16)

    def spread(row):
        return jnp.transpose(jnp.broadcast_to(row, (TOK, TOK)))

    loads[0].wait()
    loads[1].wait()
    upper = (sub <= lane).astype(F32)
    sums = lax.dot_general(
        ld_ref[...], upper, (((1,), (0,)), ((), ())),
        precision=lax.Precision.HIGHEST, preferred_element_type=F32,
    )
    doc_row = doc_ref[pl.ds(ctx, 1), :].astype(F32)
    earlier = doc_ref[pl.ds(jnp.maximum(ctx - 1, 0), 1), :].astype(F32)[:, TOK - 1 : TOK]
    before = jnp.where(ctx > 0, earlier, -1.0)
    last = doc_row[:, TOK - 1 : TOK]
    enter_row = (doc_row == before).astype(F32)
    leave_row = (doc_row == last).astype(F32)
    through = (last == before).astype(F32)
    doc_col = spread(doc_row)
    inside = (sub >= lane) & (doc_col == doc_row)
    enter_col = (doc_col == before).astype(F32)
    leave_col = (doc_col == last).astype(F32)

    def pack(state, decay, slot, dest):
        tail = state[72:96]
        rest = jnp.concatenate(
            [pltpu.roll(tail, 96, 1), pltpu.roll(tail, 64, 1), pltpu.roll(tail, 32, 1)], axis=0
        )
        full = jnp.where(wide, state[0:72], rest)
        dest[slot, 0:32] = full[0:32]
        dest[slot, 32:40] = jnp.where(low, full[32:40], decay)
        dest[slot + 1, 0:32] = full[40:72]
        dest[slot + 1, 32:40] = jnp.where(low, pltpu.roll(full[32:40], 4, 0), decay)

    def unpack(arrived, h):
        one, other = arrived[2 * h], arrived[2 * h + 1]
        full = jnp.concatenate(
            [one[0:32], jnp.where(low, one[32:40], pltpu.roll(other[32:40], 4, 0)), other[0:32]], axis=0
        )
        tail = jnp.where(
            third < 32, pltpu.roll(full[0:24], 32, 1),
            jnp.where(third < 64, pltpu.roll(full[24:48], 64, 1), pltpu.roll(full[48:72], 96, 1)),
        )
        tail = jnp.where(third < DH, tail, 0.0)
        return jnp.concatenate(
            [jnp.where(wide, full, 0.0), tail, jnp.zeros((TOK - DH, TOK), F32)], axis=0
        )

    loads[2].wait()
    loads[3].wait()
    k_heads = heads_of(k_ref)
    v_heads = heads_of(v_ref)
    passing = []
    for h in range(HEADS):
        row = sums[h : h + 1, :]
        final = row[:, TOK - 1 : TOK]
        passing.append(jnp.exp(final) * through)
        vb = v_heads[h].astype(BF16)
        vh[h] = vb
        kh[h] = k_heads[h].astype(BF16)
        kt = jnp.transpose(k_heads[h]) * (jnp.exp(final - row) * leave_row)
        update = two(nn, split(kt), vb)
        pack(update, passing[h], 2 * h, up)

    rows_near = jnp.minimum(z, 2) + jnp.minimum(ROWS - 1 - z, 2)
    pl.semaphore_wait(barrier, (ROW - 1) + (HEAD_DEVS - 1) + rows_near)

    def remote(src, dst, send_sem, recv_sem, target):
        return pltpu.make_async_remote_copy(
            src_ref=src, dst_ref=dst, send_sem=send_sem, recv_sem=recv_sem,
            device_id=target, device_id_type=MESH,
        )

    def wait_all(view, sem):
        pltpu.make_async_copy(view, view, sem).wait()

    def drain(copies):
        for condition, copy in copies:
            if condition is None:
                copy.wait_send()
            else:
                pl.when(condition)(copy.wait_send)

    def across(phase, src, dst, rows):
        for step in ORDER:
            other = lax.rem(y + step, ROW)
            copy = remote(
                src.at[other, pl.ds(0, rows)], dst.at[y, pl.ds(0, rows)],
                a_send.at[phase], a_recv.at[phase],
                (z * ROW + other, head),
            )
            copy.start()
        dst[pl.ds(y, 1)] = src[pl.ds(y, 1)]

    def arrive(phase, dst, rows):
        wait_all(dst.at[pl.ds(0, ROW - 1), pl.ds(0, rows)], a_recv.at[phase])

    def factor_of(tile):
        return jnp.broadcast_to(tile[USED : USED + 1], (PART, TOK))

    def join(near, far, factor):
        return jnp.where(data, near, 0.0) + factor * far

    def row_scan(base, forward, arrived, prefix, zo, zi, result, returned):
        arrive(base, arrived, USED + 1 if forward else USED)
        order = range(ROW) if forward else range(ROW - 1, -1, -1)
        running = jnp.where(data, 0.0, 1.0)
        for place in order:
            prefix[place] = running
            running = join(arrived[place], running, factor_of(up_in[place]))
        zo[0] = running
        sign = 1 if forward else -1
        place_z = z if forward else ROWS - 1 - z
        for n in range(3):

            @pl.when(place_z <= n)
            def _(n=n):
                zi[n] = jnp.zeros((PART, TOK), F32)

        def hop(n):
            distance = 1 if n == 0 else 2
            return remote(
                zo.at[n // 2, pl.ds(0, USED + 1)], zi.at[n, pl.ds(0, USED + 1)], z_send.at[base, n], z_recv.at[base, n],
                (at_row(sign * distance), head),
            )

        sending = (place_z < ROWS - 1, place_z < ROWS - 2, (place_z > 0) & (place_z < ROWS - 2))
        sends = []

        def send_hop(n):
            copy = hop(n)

            @pl.when(sending[n])
            def _():
                copy.start()

            sends.append((sending[n], copy))

        def get_hop(n):
            @pl.when(place_z > n)
            def _():
                hop(n).wait_recv()

        send_hop(1)
        send_hop(0)
        get_hop(0)
        get_hop(1)
        pair = join(zi[0], zi[1], factor_of(zi[0]))
        zo[1] = pair
        send_hop(2)
        get_hop(2)
        entry = pair + factor_of(pair) * zi[2]
        for step in ORDER:
            other = lax.rem(y + step, ROW)
            tile = prefix[other]
            result[pl.ds(other, 1)] = (tile + factor_of(tile) * entry)[None]
            copy = remote(
                result.at[other, pl.ds(0, USED)], returned.at[y, pl.ds(0, USED)],
                a_send.at[base + 1], a_recv.at[base + 1], (z * ROW + other, head),
            )
            copy.start()
        tile = prefix[y]
        returned[pl.ds(y, 1)] = (tile + factor_of(tile) * entry)[None]
        drain(sends)
        wait_all(result.at[pl.ds(0, ROW - 1), pl.ds(0, USED)], a_send.at[base + 1])
        arrive(base + 1, returned, USED)

    across(0, up, up_in, USED + 1)

    loads[4].wait()
    loads[5].wait()
    q_heads = heads_of(q_ref)
    g_heads = heads_of(g_ref)
    for h in range(HEADS):
        row = sums[h : h + 1, :]
        final = row[:, TOK - 1 : TOK]
        col = spread(row)
        qb = q_heads[h].astype(BF16)
        qh[h] = qb
        gh[h] = g_heads[h].astype(BF16)
        qt[h] = jnp.transpose(q_heads[h]) * (jnp.exp(row) * enter_row * FACTOR)
        ent[h] = jnp.exp(col) * enter_col * FACTOR
        leave[h] = jnp.exp(final - col) * leave_col
        weight = jnp.where(inside, jnp.exp(jnp.minimum(col - row, 0.0)), 0.0)
        within[h] = weight
        scores = weight * (nt(qb, kh[h]) * FACTOR)
        score[h] = scores
        out[h] = two(nn, split(scores), vh[h])

    wait_all(up.at[pl.ds(0, ROW - 1), pl.ds(0, USED + 1)], a_send.at[0])
    row_scan(0, True, up_in, part, zout, zin, back, back_in)

    squares = jnp.zeros((TOK, TOK), F32)
    dots = jnp.zeros((TOK, TOK), F32)
    for h in range(HEADS):
        pair = split(unpack(back_in, h))
        state_hi[h] = pair[0]
        state_lo[h] = pair[1]
        now = out[h] + ent[h] * two_right(nn, qh[h], pair)
        out[h] = now
        squares = squares + now * now
        dots = dots + now * gh[h].astype(F32)
    square_row = jnp.sum(jnp.transpose(squares), axis=0, keepdims=True)
    dot_row = jnp.sum(jnp.transpose(dots), axis=0, keepdims=True)
    small = lax.broadcasted_iota(jnp.int32, (8, TOK), 0)
    tile = jnp.where(small == 0, square_row, dot_row)
    hsend[...] = tile
    for step in range(1, HEAD_DEVS):
        other = lax.rem(head + step, HEAD_DEVS)
        copy = remote(hsend.at[pl.ds(0, 2)], hrecv.at[head, pl.ds(0, 2)], h_send, h_recv, (ctx, other))
        copy.start()
    hrecv[pl.ds(head, 1)] = tile[None]
    for h in range(HEADS):
        pair = split(out[h])
        out_hi[h] = pair[0]
        out_lo[h] = pair[1]
    wait_all(hrecv.at[pl.ds(0, HEAD_DEVS - 1), pl.ds(0, 2)], h_send)
    wait_all(hrecv.at[pl.ds(0, HEAD_DEVS - 1), pl.ds(0, 2)], h_recv)
    total = hrecv[0, 0:2]
    for slot in range(1, HEAD_DEVS):
        total = total + hrecv[slot, 0:2]
    rscale = lax.rsqrt(total[0:1] / FULL + EPS)
    drift = rscale * rscale * rscale * total[1:2] / FULL

    for h in range(HEADS):
        near = split(qt[h] * rscale)
        far = split(qt[h] * drift)
        pulled = two(nn, near, gh[h]) - three(nn, far, (out_hi[h], out_lo[h]))
        pack(pulled, passing[h], 2 * h, upb)

    across(2, upb, upb_in, USED)

    rscale_col = spread(rscale)
    drift_col = spread(drift)
    normed = []
    grads = []
    for h in range(HEADS):
        now = out[h]
        normed.append(now * rscale_col)
        grad_pair = split(rscale_col * gh[h].astype(F32) - drift_col * now)
        mixed = within[h] * two(nt, grad_pair, vh[h])
        grads.append(
            FACTOR * two(nn, split(mixed), kh[h])
            + ent[h] * three(nt, grad_pair, (state_hi[h], state_lo[h]))
        )
        dkl[h] = FACTOR * two(nn, split(jnp.transpose(mixed)), qh[h])
        dvl[h] = three(nn, split(jnp.transpose(score[h])), grad_pair)
    put_heads(att_ref, normed)
    put_heads(dq_ref, grads)

    wait_all(upb.at[pl.ds(0, ROW - 1), pl.ds(0, USED)], a_send.at[2])
    row_scan(2, False, upb_in, partb, zoutb, zinb, backb, backb_in)

    state_pairs = [split(unpack(backb_in, h)) for h in range(HEADS)]
    put_heads(
        dk_ref, [dkl[h] + leave[h] * two_right(nt, vh[h], state_pairs[h]) for h in range(HEADS)]
    )
    put_heads(
        dv_ref, [dvl[h] + leave[h] * two_right(nn, kh[h], state_pairs[h]) for h in range(HEADS)]
    )


def write(*refs):
    srcs, dsts, sem = refs[0:4], refs[4:8], refs[8]
    copies = [pltpu.make_async_copy(a, b, sem.at[n]) for n, (a, b) in enumerate(zip(srcs, dsts))]
    for copy in copies:
        copy.start()
    for copy in copies:
        copy.wait()


def local(queries, key_vectors, value_vectors, out_grad, log_decay, doc_ids):
    square_bf = pltpu.VMEM((HEADS, TOK, TOK), BF16)
    square_f = pltpu.VMEM((HEADS, TOK, TOK), F32)
    slices = pltpu.VMEM((ROW, PART, TOK), F32)
    scan = [slices] * 5 + [pltpu.VMEM((2, PART, TOK), F32), pltpu.VMEM((3, PART, TOK), F32)]
    dma = pltpu.SemaphoreType.DMA
    result = jax.ShapeDtypeStruct((TOK, WIDTH), BF16)
    vmem = pl.BlockSpec(memory_space=pltpu.VMEM)
    hbm = pl.BlockSpec(memory_space=pltpu.HBM)
    queries, key_vectors, value_vectors, out_grad, log_decay, docs = (
        pltpu.with_memory_space_constraint(x, pltpu.HBM)
        for x in (
            queries, key_vectors, value_vectors, out_grad, log_decay,
            doc_ids.reshape(ROW * ROWS, TOK),
        )
    )
    results = pl.pallas_call(
        kernel,
        out_shape=[result] * 4,
        in_specs=[hbm] * 6,
        out_specs=[vmem] * 4,
        scratch_shapes=[pltpu.VMEM((TOK, WIDTH), BF16)] * 4
        + [pltpu.VMEM((HEADS, TOK), F32), pltpu.VMEM((ROW * ROWS, TOK), jnp.int32), dma((6,))]
        + [square_bf] * 4
        + [square_f] * 6
        + [square_bf] * 4
        + [square_f] * 2
        + scan * 2
        + [pltpu.VMEM((8, TOK), F32), pltpu.VMEM((HEAD_DEVS, 8, TOK), F32)]
        + [dma((4,)), dma((4,)), dma((4, 3)), dma((4, 3)), dma, dma],
        compiler_params=pltpu.CompilerParams(
            collective_id=0, has_side_effects=True, vmem_limit_bytes=32 << 20
        ),
    )(
        queries, key_vectors, value_vectors, out_grad, log_decay, docs,
    )
    return pl.pallas_call(
        write,
        out_shape=[result] * 4,
        in_specs=[vmem] * 4,
        out_specs=[hbm] * 4,
        scratch_shapes=[dma((4,))],
    )(*(pltpu.with_memory_space_constraint(x, pltpu.VMEM) for x in results))


def solution(mesh):
    return jax.shard_map(
        local,
        mesh=mesh,
        in_specs=(
            P("ctx", "head"), P("ctx", "head"), P("ctx", "head"), P("ctx", "head"),
            P("head", "ctx"), P(),
        ),
        out_specs=(P("ctx", "head"),) * 4,
        check_vma=False,
    )
```

```python
import jax
import jax.numpy as jnp
from jax import lax
from jax.experimental import pallas as pl
from jax.experimental.pallas import tpu as pltpu
from jax.sharding import PartitionSpec as P

HEADS = 4
DH = 96
TOK = 128
WIDTH = HEADS * DH
FULL = 3072
ROW = 8
ROWS = 12
HEAD_DEVS = 8
PART = 40
USED = 36
CUT = 24
ORDER = (4, 3, 5, 2, 6, 1, 7)
EPS = 1e-05
FACTOR = DH ** (-0.5)
F32 = jnp.float32
BF16 = jnp.bfloat16
MESH = pl.DeviceIdType.MESH


def nn(a, b):
    return lax.dot_general(a, b, (((1,), (0,)), ((), ())), preferred_element_type=F32)


def nt(a, b):
    return lax.dot_general(a, b, (((1,), (1,)), ((), ())), preferred_element_type=F32)


def split(x):
    hi = x.astype(BF16)
    return hi, (x - hi.astype(F32)).astype(BF16)


def two(dot, a, b):
    return dot(a[0], b) + dot(a[1], b)


def two_right(dot, a, b):
    return dot(a, b[0]) + dot(a, b[1])


def three(dot, a, b):
    return dot(a[0], b[0]) + (dot(a[0], b[1]) + dot(a[1], b[0]))


def kernel(
    q_hbm, k_hbm, v_hbm, g_hbm, ld_hbm, doc_hbm,
    att_ref, dq_ref, dk_ref, dv_ref,
    q_ref, k_ref, v_ref, g_ref, ld_ref, doc_ref, in_sem,
    qh, kh, vh, gh, qt, within, score, ent, leave, out, state_hi, state_lo,
    out_hi, out_lo, dkl, dvl,
    up, up_in, part, back, back_in, zout, zin,
    upb, upb_in, partb, backb, backb_in, zoutb, zinb,
    hsend, hrecv,
    a_send, a_recv, z_send, z_recv, h_send, h_recv,
):
    ctx = lax.axis_index("ctx")
    head = lax.axis_index("head")
    y = lax.rem(ctx, ROW)
    z = ctx // ROW

    def at_row(step):
        return lax.rem(z + step + ROWS, ROWS) * ROW + y

    barrier = pltpu.get_barrier_semaphore()
    for step in range(1, ROW):
        pl.semaphore_signal(
            barrier, inc=1, device_id=(z * ROW + lax.rem(y + step, ROW), head), device_id_type=MESH
        )
    for step in (-2, -1, 1, 2):

        @pl.when((z + step >= 0) & (z + step < ROWS))
        def _(step=step):
            pl.semaphore_signal(barrier, inc=1, device_id=(at_row(step), head), device_id_type=MESH)

    for step in range(1, HEAD_DEVS):
        pl.semaphore_signal(
            barrier, inc=1, device_id=(ctx, lax.rem(head + step, HEAD_DEVS)), device_id_type=MESH
        )

    loads = [
        pltpu.make_async_copy(src, dst, in_sem.at[n])
        for n, (src, dst) in enumerate((
            (ld_hbm, ld_ref), (doc_hbm, doc_ref), (k_hbm, k_ref),
            (v_hbm, v_ref), (q_hbm, q_ref), (g_hbm, g_ref),
        ))
    ]
    for load in loads:
        load.start()

    lane = lax.broadcasted_iota(jnp.int32, (TOK, TOK), 1)
    sub = lax.broadcasted_iota(jnp.int32, (TOK, TOK), 0)
    real = lane < DH
    data = lax.broadcasted_iota(jnp.int32, (PART - CUT, TOK), 0) < USED - CUT
    wide = lax.broadcasted_iota(jnp.int32, (72, TOK), 1) < DH
    third = lax.broadcasted_iota(jnp.int32, (24, TOK), 1)
    low = lax.broadcasted_iota(jnp.int32, (8, TOK), 0) < 4

    def heads_of(ref):
        tiles = [ref[:, TOK * t : TOK * t + TOK].astype(F32) for t in range(3)]
        zero = jnp.zeros((TOK, TOK), F32)
        h0 = tiles[0]
        h1 = pltpu.roll(jnp.where(lane >= 96, tiles[0], tiles[1]), 32, 1)
        h2 = pltpu.roll(jnp.where(lane >= 64, tiles[1], tiles[2]), 64, 1)
        h3 = pltpu.roll(tiles[2], 96, 1)
        return [jnp.where(real, h, zero) for h in (h0, h1, h2, h3)]

    def put_heads(ref, parts):
        r1 = pltpu.roll(parts[1], 96, 1)
        r2 = pltpu.roll(parts[2], 64, 1)
        r3 = pltpu.roll(parts[3], 32, 1)
        ref[:, 0:TOK] = jnp.where(lane < 96, parts[0], r1).astype(BF16)
        ref[:, TOK : 2 * TOK] = jnp.where(lane < 64, r1, r2).astype(BF16)
        ref[:, 2 * TOK : 3 * TOK] = jnp.where(lane < 32, r2, r3).astype(BF16)

    def spread(row):
        return jnp.transpose(jnp.broadcast_to(row, (TOK, TOK)))

    loads[0].wait()
    loads[1].wait()
    upper = (sub <= lane).astype(F32)
    sums = lax.dot_general(
        ld_ref[...], upper, (((1,), (0,)), ((), ())),
        precision=lax.Precision.HIGHEST, preferred_element_type=F32,
    )
    doc_row = doc_ref[pl.ds(ctx, 1), :].astype(F32)
    earlier = doc_ref[pl.ds(jnp.maximum(ctx - 1, 0), 1), :].astype(F32)[:, TOK - 1 : TOK]
    before = jnp.where(ctx > 0, earlier, -1.0)
    last = doc_row[:, TOK - 1 : TOK]
    enter_row = (doc_row == before).astype(F32)
    leave_row = (doc_row == last).astype(F32)
    through = (last == before).astype(F32)
    doc_col = spread(doc_row)
    inside = (sub >= lane) & (doc_col == doc_row)
    enter_col = (doc_col == before).astype(F32)
    leave_col = (doc_col == last).astype(F32)

    def pack(state, decay, slot, dest):
        tail = state[72:96]
        rest = jnp.concatenate(
            [pltpu.roll(tail, 96, 1), pltpu.roll(tail, 64, 1), pltpu.roll(tail, 32, 1)], axis=0
        )
        full = jnp.where(wide, state[0:72], rest)
        dest[slot, 0:32] = full[0:32]
        dest[slot, 32:40] = jnp.where(low, full[32:40], decay)
        dest[slot + 1, 0:32] = full[40:72]
        dest[slot + 1, 32:40] = jnp.where(low, pltpu.roll(full[32:40], 4, 0), decay)

    def unpack(arrived, h):
        one, other = arrived[2 * h], arrived[2 * h + 1]
        full = jnp.concatenate(
            [one[0:32], jnp.where(low, one[32:40], pltpu.roll(other[32:40], 4, 0)), other[0:32]], axis=0
        )
        tail = jnp.where(
            third < 32, pltpu.roll(full[0:24], 32, 1),
            jnp.where(third < 64, pltpu.roll(full[24:48], 64, 1), pltpu.roll(full[48:72], 96, 1)),
        )
        tail = jnp.where(third < DH, tail, 0.0)
        return jnp.concatenate(
            [jnp.where(wide, full, 0.0), tail, jnp.zeros((TOK - DH, TOK), F32)], axis=0
        )

    loads[2].wait()
    loads[3].wait()
    k_heads = heads_of(k_ref)
    v_heads = heads_of(v_ref)
    passing = []
    for h in range(HEADS):
        row = sums[h : h + 1, :]
        final = row[:, TOK - 1 : TOK]
        passing.append(jnp.exp(final) * through)
        vb = v_heads[h].astype(BF16)
        vh[h] = vb
        kh[h] = k_heads[h].astype(BF16)
        kt = jnp.transpose(k_heads[h]) * (jnp.exp(final - row) * leave_row)
        update = two(nn, split(kt), vb)
        pack(update, passing[h], 2 * h, up)

    rows_near = jnp.minimum(z, 2) + jnp.minimum(ROWS - 1 - z, 2)
    pl.semaphore_wait(barrier, (ROW - 1) + (HEAD_DEVS - 1) + rows_near)

    def remote(src, dst, send_sem, recv_sem, target):
        return pltpu.make_async_remote_copy(
            src_ref=src, dst_ref=dst, send_sem=send_sem, recv_sem=recv_sem,
            device_id=target, device_id_type=MESH,
        )

    def wait_all(view, sem):
        pltpu.make_async_copy(view, view, sem).wait()

    def drain(copies):
        for condition, copy in copies:
            if condition is None:
                copy.wait_send()
            else:
                pl.when(condition)(copy.wait_send)

    def pieces(last):
        return (pl.ds(CUT, last - CUT), pl.ds(0, CUT))

    def across(phase, src, dst, last):
        for n, rows in enumerate(pieces(last)):
            for step in ORDER:
                other = lax.rem(y + step, ROW)
                remote(
                    src.at[other, rows], dst.at[y, rows], a_send.at[phase], a_recv.at[phase, n],
                    (z * ROW + other, head),
                ).start()
        dst[pl.ds(y, 1)] = src[pl.ds(y, 1)]

    def factor_of(ref, place, rows):
        return jnp.broadcast_to(ref[place, USED : USED + 1], (rows, TOK))

    def row_scan(base, forward, arrived, prefix, zo, zi, result, returned):
        order = range(ROW) if forward else range(ROW - 1, -1, -1)
        sign = 1 if forward else -1
        place_z = z if forward else ROWS - 1 - z
        sending = (place_z < ROWS - 1, place_z < ROWS - 2, (place_z > 0) & (place_z < ROWS - 2))
        spans = pieces(USED + 1)
        tiles = (slice(CUT, PART), slice(0, CUT))
        heights = (PART - CUT, CUT)
        sends = []

        def hop(n, piece):
            distance = 1 if n == 0 else 2
            return remote(
                zo.at[n // 2, spans[piece]], zi.at[n, spans[piece]],
                z_send.at[base + piece, n], z_recv.at[base + piece, n],
                (at_row(sign * distance), head),
            )

        def send_hop(n, piece):
            copy = hop(n, piece)
            pl.when(sending[n])(copy.start)
            sends.append((sending[n], copy))

        def get_hop(n, piece):
            pl.when(place_z > n)(hop(n, piece).wait_recv)

        def near_part(tile, piece):
            return jnp.where(data, tile, 0.0) if piece == 0 else tile

        for n in range(3):

            @pl.when(place_z <= n)
            def _(n=n):
                zi[n] = jnp.zeros((PART, TOK), F32)

        for piece in range(2):
            rows = tiles[piece]
            count = (USED + 1 if forward else USED) - CUT if piece == 0 else CUT
            wait_all(
                arrived.at[pl.ds(0, ROW - 1), pl.ds(CUT if piece == 0 else 0, count)],
                a_recv.at[base, piece],
            )
            running = jnp.where(data, 0.0, 1.0) if piece == 0 else jnp.zeros((CUT, TOK), F32)
            for place in order:
                prefix[place, rows] = running
                running = near_part(arrived[place, rows], piece) + (
                    factor_of(up_in, place, heights[piece]) * running
                )
            zo[0, rows] = running
            send_hop(1, piece)
            send_hop(0, piece)
        for piece in range(2):
            rows = tiles[piece]
            get_hop(0, piece)
            get_hop(1, piece)
            zo[1, rows] = near_part(zi[0, rows], piece) + (
                factor_of(zi, 0, heights[piece]) * zi[1, rows]
            )
            send_hop(2, piece)
        returning = pieces(USED)
        for piece in range(2):
            rows = tiles[piece]
            get_hop(2, piece)
            entry = zo[1, rows] + factor_of(zo, 1, heights[piece]) * zi[2, rows]
            for step in ORDER:
                other = lax.rem(y + step, ROW)
                result[other, rows] = (
                    prefix[other, rows] + factor_of(prefix, other, heights[piece]) * entry
                )
                remote(
                    result.at[other, returning[piece]], returned.at[y, returning[piece]],
                    a_send.at[base + 1], a_recv.at[base + 1, 0], (z * ROW + other, head),
                ).start()
            returned[y, rows] = prefix[y, rows] + factor_of(prefix, y, heights[piece]) * entry
        drain(sends)
        whole = pl.ds(0, USED)
        wait_all(result.at[pl.ds(0, ROW - 1), whole], a_send.at[base + 1])
        wait_all(returned.at[pl.ds(0, ROW - 1), whole], a_recv.at[base + 1, 0])

    across(0, up, up_in, USED + 1)

    loads[4].wait()
    loads[5].wait()
    q_heads = heads_of(q_ref)
    g_heads = heads_of(g_ref)
    for h in range(HEADS):
        row = sums[h : h + 1, :]
        final = row[:, TOK - 1 : TOK]
        col = spread(row)
        qb = q_heads[h].astype(BF16)
        qh[h] = qb
        gh[h] = g_heads[h].astype(BF16)
        qt[h] = jnp.transpose(q_heads[h]) * (jnp.exp(row) * enter_row * FACTOR)
        ent[h] = jnp.exp(col) * enter_col * FACTOR
        leave[h] = jnp.exp(final - col) * leave_col
        weight = jnp.where(inside, jnp.exp(jnp.minimum(col - row, 0.0)), 0.0)
        within[h] = weight
        scores = weight * (nt(qb, kh[h]) * FACTOR)
        score[h] = scores
        out[h] = two(nn, split(scores), vh[h])

    wait_all(up.at[pl.ds(0, ROW - 1), pl.ds(0, USED + 1)], a_send.at[0])
    row_scan(0, True, up_in, part, zout, zin, back, back_in)

    squares = jnp.zeros((TOK, TOK), F32)
    dots = jnp.zeros((TOK, TOK), F32)
    for h in range(HEADS):
        pair = split(unpack(back_in, h))
        state_hi[h] = pair[0]
        state_lo[h] = pair[1]
        now = out[h] + ent[h] * two_right(nn, qh[h], pair)
        out[h] = now
        squares = squares + now * now
        dots = dots + now * gh[h].astype(F32)
    square_row = jnp.sum(jnp.transpose(squares), axis=0, keepdims=True)
    dot_row = jnp.sum(jnp.transpose(dots), axis=0, keepdims=True)
    small = lax.broadcasted_iota(jnp.int32, (8, TOK), 0)
    tile = jnp.where(small == 0, square_row, dot_row)
    hsend[...] = tile
    for step in range(1, HEAD_DEVS):
        other = lax.rem(head + step, HEAD_DEVS)
        copy = remote(hsend.at[pl.ds(0, 2)], hrecv.at[head, pl.ds(0, 2)], h_send, h_recv, (ctx, other))
        copy.start()
    hrecv[pl.ds(head, 1)] = tile[None]
    for h in range(HEADS):
        pair = split(out[h])
        out_hi[h] = pair[0]
        out_lo[h] = pair[1]
    wait_all(hrecv.at[pl.ds(0, HEAD_DEVS - 1), pl.ds(0, 2)], h_send)
    wait_all(hrecv.at[pl.ds(0, HEAD_DEVS - 1), pl.ds(0, 2)], h_recv)
    total = hrecv[0, 0:2]
    for slot in range(1, HEAD_DEVS):
        total = total + hrecv[slot, 0:2]
    rscale = lax.rsqrt(total[0:1] / FULL + EPS)
    drift = rscale * rscale * rscale * total[1:2] / FULL

    for h in range(HEADS):
        near = split(qt[h] * rscale)
        far = split(qt[h] * drift)
        pulled = two(nn, near, gh[h]) - three(nn, far, (out_hi[h], out_lo[h]))
        pack(pulled, passing[h], 2 * h, upb)

    across(2, upb, upb_in, USED)

    rscale_col = spread(rscale)
    drift_col = spread(drift)
    normed = []
    grads = []
    for h in range(HEADS):
        now = out[h]
        normed.append(now * rscale_col)
        grad_pair = split(rscale_col * gh[h].astype(F32) - drift_col * now)
        mixed = within[h] * two(nt, grad_pair, vh[h])
        grads.append(
            FACTOR * two(nn, split(mixed), kh[h])
            + ent[h] * three(nt, grad_pair, (state_hi[h], state_lo[h]))
        )
        dkl[h] = FACTOR * two(nn, split(jnp.transpose(mixed)), qh[h])
        dvl[h] = three(nn, split(jnp.transpose(score[h])), grad_pair)
    put_heads(att_ref, normed)
    put_heads(dq_ref, grads)

    wait_all(upb.at[pl.ds(0, ROW - 1), pl.ds(0, USED)], a_send.at[2])
    row_scan(2, False, upb_in, partb, zoutb, zinb, backb, backb_in)

    state_pairs = [split(unpack(backb_in, h)) for h in range(HEADS)]
    put_heads(
        dk_ref, [dkl[h] + leave[h] * two_right(nt, vh[h], state_pairs[h]) for h in range(HEADS)]
    )
    put_heads(
        dv_ref, [dvl[h] + leave[h] * two_right(nn, kh[h], state_pairs[h]) for h in range(HEADS)]
    )


def write(*refs):
    srcs, dsts, sem = refs[0:4], refs[4:8], refs[8]
    copies = [pltpu.make_async_copy(a, b, sem.at[n]) for n, (a, b) in enumerate(zip(srcs, dsts))]
    for copy in copies:
        copy.start()
    for copy in copies:
        copy.wait()


def local(queries, key_vectors, value_vectors, out_grad, log_decay, doc_ids):
    square_bf = pltpu.VMEM((HEADS, TOK, TOK), BF16)
    square_f = pltpu.VMEM((HEADS, TOK, TOK), F32)
    slices = pltpu.VMEM((ROW, PART, TOK), F32)
    scan = [slices] * 5 + [pltpu.VMEM((2, PART, TOK), F32), pltpu.VMEM((3, PART, TOK), F32)]
    dma = pltpu.SemaphoreType.DMA
    result = jax.ShapeDtypeStruct((TOK, WIDTH), BF16)
    vmem = pl.BlockSpec(memory_space=pltpu.VMEM)
    hbm = pl.BlockSpec(memory_space=pltpu.HBM)
    queries, key_vectors, value_vectors, out_grad, log_decay, docs = (
        pltpu.with_memory_space_constraint(x, pltpu.HBM)
        for x in (
            queries, key_vectors, value_vectors, out_grad, log_decay,
            doc_ids.reshape(ROW * ROWS, TOK),
        )
    )
    results = pl.pallas_call(
        kernel,
        out_shape=[result] * 4,
        in_specs=[hbm] * 6,
        out_specs=[vmem] * 4,
        scratch_shapes=[pltpu.VMEM((TOK, WIDTH), BF16)] * 4
        + [pltpu.VMEM((HEADS, TOK), F32), pltpu.VMEM((ROW * ROWS, TOK), jnp.int32), dma((6,))]
        + [square_bf] * 4
        + [square_f] * 6
        + [square_bf] * 4
        + [square_f] * 2
        + scan * 2
        + [pltpu.VMEM((8, TOK), F32), pltpu.VMEM((HEAD_DEVS, 8, TOK), F32)]
        + [dma((4,)), dma((4, 2)), dma((4, 3)), dma((4, 3)), dma, dma],
        compiler_params=pltpu.CompilerParams(
            collective_id=0, has_side_effects=True, vmem_limit_bytes=32 << 20
        ),
    )(
        queries, key_vectors, value_vectors, out_grad, log_decay, docs,
    )
    return pl.pallas_call(
        write,
        out_shape=[result] * 4,
        in_specs=[vmem] * 4,
        out_specs=[hbm] * 4,
        scratch_shapes=[dma((4,))],
    )(*(pltpu.with_memory_space_constraint(x, pltpu.VMEM) for x in results))


def solution(mesh):
    return jax.shard_map(
        local,
        mesh=mesh,
        in_specs=(
            P("ctx", "head"), P("ctx", "head"), P("ctx", "head"), P("ctx", "head"),
            P("head", "ctx"), P(),
        ),
        out_specs=(P("ctx", "head"),) * 4,
        check_vma=False,
    )
```

```python
import jax
import jax.numpy as jnp
from jax import lax
from jax.experimental import pallas as pl
from jax.experimental.pallas import tpu as pltpu
from jax.sharding import PartitionSpec as P

HEADS = 4
DH = 96
TOK = 128
WIDTH = HEADS * DH
FULL = 3072
ROW = 8
ROWS = 12
HEAD_DEVS = 8
PART = 40
USED = 36
SPLIT = 4
CUT = 24
ORDER = (4, 3, 5, 2, 6, 1, 7)
EPS = 1e-05
FACTOR = DH ** (-0.5)
F32 = jnp.float32
BF16 = jnp.bfloat16
MESH = pl.DeviceIdType.MESH


def nn(a, b):
    return lax.dot_general(a, b, (((1,), (0,)), ((), ())), preferred_element_type=F32)


def nt(a, b):
    return lax.dot_general(a, b, (((1,), (1,)), ((), ())), preferred_element_type=F32)


def split(x):
    hi = x.astype(BF16)
    return hi, (x - hi.astype(F32)).astype(BF16)


def two(dot, a, b):
    return dot(a[0], b) + dot(a[1], b)


def two_right(dot, a, b):
    return dot(a, b[0]) + dot(a, b[1])


def three(dot, a, b):
    return dot(a[0], b[0]) + (dot(a[0], b[1]) + dot(a[1], b[0]))


def kernel(
    q_hbm, k_hbm, v_hbm, g_hbm, ld_hbm, doc_hbm,
    att_ref, dq_ref, dk_ref, dv_ref,
    q_ref, k_ref, v_ref, g_ref, ld_ref, doc_ref, in_sem,
    qh, kh, vh, gh, qt, within, score, ent, leave, out, state_hi, state_lo,
    out_hi, out_lo, dkl, dvl,
    up, up_in, part, back, back_in, zout, zin,
    upb, upb_in, partb, backb, backb_in, zoutb, zinb,
    hsend, hrecv,
    a_send, a_recv, z_send, z_recv, h_send, h_recv,
):
    ctx = lax.axis_index("ctx")
    head = lax.axis_index("head")
    y = lax.rem(ctx, ROW)
    z = ctx // ROW

    def at_row(step):
        return lax.rem(z + step + ROWS, ROWS) * ROW + y

    barrier = pltpu.get_barrier_semaphore()
    for step in ORDER:
        pl.semaphore_signal(
            barrier, inc=1, device_id=(z * ROW + lax.rem(y + step, ROW), head), device_id_type=MESH
        )
    for step in (-2, -1, 1, 2):

        @pl.when((z + step >= 0) & (z + step < ROWS))
        def _(step=step):
            pl.semaphore_signal(barrier, inc=1, device_id=(at_row(step), head), device_id_type=MESH)

    for step in range(1, HEAD_DEVS):
        pl.semaphore_signal(
            barrier, inc=1, device_id=(ctx, lax.rem(head + step, HEAD_DEVS)), device_id_type=MESH
        )

    loads = [
        pltpu.make_async_copy(src, dst, in_sem.at[n])
        for n, (src, dst) in enumerate((
            (ld_hbm, ld_ref), (doc_hbm.at[pl.ds(ctx, 1)], doc_ref.at[pl.ds(1, 1)]),
            (k_hbm, k_ref), (v_hbm, v_ref), (q_hbm, q_ref), (g_hbm, g_ref),
            (doc_hbm.at[pl.ds(jnp.maximum(ctx - 1, 0), 1)], doc_ref.at[pl.ds(0, 1)]),
        ))
    ]
    for n in (0, 1, 6):
        loads[n].start()
    for n, (src, dst) in enumerate(((k_hbm, k_ref), (v_hbm, v_ref), (q_hbm, q_ref), (g_hbm, g_ref))):
        for cut in range(SPLIT):
            rows = pl.ds(TOK // SPLIT * cut, TOK // SPLIT)
            pltpu.make_async_copy(src.at[rows], dst.at[rows], in_sem.at[n + 2]).start()

    lane = lax.broadcasted_iota(jnp.int32, (TOK, TOK), 1)
    sub = lax.broadcasted_iota(jnp.int32, (TOK, TOK), 0)
    real = lane < DH
    data = lax.broadcasted_iota(jnp.int32, (PART - CUT, TOK), 0) < USED - CUT
    wide = lax.broadcasted_iota(jnp.int32, (72, TOK), 1) < DH
    third = lax.broadcasted_iota(jnp.int32, (24, TOK), 1)
    low = lax.broadcasted_iota(jnp.int32, (8, TOK), 0) < 4

    def heads_of(ref):
        tiles = [ref[:, TOK * t : TOK * t + TOK].astype(F32) for t in range(3)]
        zero = jnp.zeros((TOK, TOK), F32)
        h0 = tiles[0]
        h1 = pltpu.roll(jnp.where(lane >= 96, tiles[0], tiles[1]), 32, 1)
        h2 = pltpu.roll(jnp.where(lane >= 64, tiles[1], tiles[2]), 64, 1)
        h3 = pltpu.roll(tiles[2], 96, 1)
        return [jnp.where(real, h, zero) for h in (h0, h1, h2, h3)]

    def put_heads(ref, parts):
        r1 = pltpu.roll(parts[1], 96, 1)
        r2 = pltpu.roll(parts[2], 64, 1)
        r3 = pltpu.roll(parts[3], 32, 1)
        ref[:, 0:TOK] = jnp.where(lane < 96, parts[0], r1).astype(BF16)
        ref[:, TOK : 2 * TOK] = jnp.where(lane < 64, r1, r2).astype(BF16)
        ref[:, 2 * TOK : 3 * TOK] = jnp.where(lane < 32, r2, r3).astype(BF16)

    def spread(row):
        return jnp.transpose(jnp.broadcast_to(row, (TOK, TOK)))

    loads[0].wait()
    loads[1].wait()
    loads[6].wait()
    upper = (sub <= lane).astype(F32)
    sums = lax.dot_general(
        ld_ref[...], upper, (((1,), (0,)), ((), ())),
        precision=lax.Precision.HIGHEST, preferred_element_type=F32,
    )
    doc_row = doc_ref[1:2, :].astype(F32)
    earlier = doc_ref[0:1, TOK - 1 : TOK].astype(F32)
    before = jnp.where(ctx > 0, earlier, -1.0)
    last = doc_row[:, TOK - 1 : TOK]
    enter_row = (doc_row == before).astype(F32)
    leave_row = (doc_row == last).astype(F32)
    through = (last == before).astype(F32)

    def pack(state, decay, slot, dest):
        tail = state[72:96]
        rest = jnp.concatenate(
            [pltpu.roll(tail, 96, 1), pltpu.roll(tail, 64, 1), pltpu.roll(tail, 32, 1)], axis=0
        )
        full = jnp.where(wide, state[0:72], rest)
        dest[slot, 0:32] = full[0:32]
        dest[slot, 32:40] = jnp.where(low, full[32:40], decay)
        dest[slot + 1, 0:32] = full[40:72]
        dest[slot + 1, 32:40] = jnp.where(low, pltpu.roll(full[32:40], 4, 0), decay)

    def unpack(arrived, h):
        one, other = arrived[2 * h], arrived[2 * h + 1]
        full = jnp.concatenate(
            [one[0:32], jnp.where(low, one[32:40], pltpu.roll(other[32:40], 4, 0)), other[0:32]], axis=0
        )
        tail = jnp.where(
            third < 32, pltpu.roll(full[0:24], 32, 1),
            jnp.where(third < 64, pltpu.roll(full[24:48], 64, 1), pltpu.roll(full[48:72], 96, 1)),
        )
        tail = jnp.where(third < DH, tail, 0.0)
        return jnp.concatenate(
            [jnp.where(wide, full, 0.0), tail, jnp.zeros((TOK - DH, TOK), F32)], axis=0
        )

    loads[2].wait()
    loads[3].wait()
    k_heads = heads_of(k_ref)
    v_heads = heads_of(v_ref)
    passing = []
    for h in range(HEADS):
        row = sums[h : h + 1, :]
        final = row[:, TOK - 1 : TOK]
        passing.append(jnp.exp(final) * through)
        vb = v_heads[h].astype(BF16)
        vh[h] = vb
        kh[h] = k_heads[h].astype(BF16)
        kt = jnp.transpose(k_heads[h]) * (jnp.exp(final - row) * leave_row)
        update = two(nn, split(kt), vb)
        pack(update, passing[h], 2 * h, up)

    rows_near = jnp.minimum(z, 2) + jnp.minimum(ROWS - 1 - z, 2)
    pl.semaphore_wait(barrier, (ROW - 1) + (HEAD_DEVS - 1) + rows_near)

    def remote(src, dst, send_sem, recv_sem, target):
        return pltpu.make_async_remote_copy(
            src_ref=src, dst_ref=dst, send_sem=send_sem, recv_sem=recv_sem,
            device_id=target, device_id_type=MESH,
        )

    def wait_all(view, sem):
        pltpu.make_async_copy(view, view, sem).wait()

    def drain(copies):
        for condition, copy in copies:
            if condition is None:
                copy.wait_send()
            else:
                pl.when(condition)(copy.wait_send)

    def pieces(last):
        return (pl.ds(CUT, last - CUT), pl.ds(0, CUT))

    def across(phase, src, dst, last):
        for n, rows in enumerate(pieces(last)):
            for step in ORDER:
                other = lax.rem(y + step, ROW)
                remote(
                    src.at[other, rows], dst.at[y, rows], a_send.at[phase], a_recv.at[phase, n],
                    (z * ROW + other, head),
                ).start()
        dst[pl.ds(y, 1)] = src[pl.ds(y, 1)]

    def factor_of(ref, place, rows):
        return jnp.broadcast_to(ref[place, USED : USED + 1], (rows, TOK))

    def row_scan(base, forward, arrived, prefix, zo, zi, result, returned):
        order = range(ROW) if forward else range(ROW - 1, -1, -1)
        sign = 1 if forward else -1
        place_z = z if forward else ROWS - 1 - z
        sending = (place_z < ROWS - 1, place_z < ROWS - 2, (place_z > 0) & (place_z < ROWS - 2))
        spans = pieces(USED + 1)
        tiles = (slice(CUT, PART), slice(0, CUT))
        heights = (PART - CUT, CUT)
        sends = []

        def hop(n, piece):
            distance = 1 if n == 0 else 2
            return remote(
                zo.at[n // 2, spans[piece]], zi.at[n, spans[piece]],
                z_send.at[base + piece, n], z_recv.at[base + piece, n],
                (at_row(sign * distance), head),
            )

        def send_hop(n, piece):
            copy = hop(n, piece)
            pl.when(sending[n])(copy.start)
            sends.append((sending[n], copy))

        def get_hop(n, piece):
            pl.when(place_z > n)(hop(n, piece).wait_recv)

        def near_part(tile, piece):
            return jnp.where(data, tile, 0.0) if piece == 0 else tile

        for n in range(3):

            @pl.when(place_z <= n)
            def _(n=n):
                zi[n] = jnp.zeros((PART, TOK), F32)

        for piece in range(2):
            rows = tiles[piece]
            count = (USED + 1 if forward else USED) - CUT if piece == 0 else CUT
            wait_all(
                arrived.at[pl.ds(0, ROW - 1), pl.ds(CUT if piece == 0 else 0, count)],
                a_recv.at[base, piece],
            )
            running = jnp.where(data, 0.0, 1.0) if piece == 0 else jnp.zeros((CUT, TOK), F32)
            for place in order:
                prefix[place, rows] = running
                running = near_part(arrived[place, rows], piece) + (
                    factor_of(up_in, place, heights[piece]) * running
                )
            zo[0, rows] = running
            send_hop(1, piece)
            send_hop(0, piece)
        for piece in range(2):
            rows = tiles[piece]
            get_hop(0, piece)
            get_hop(1, piece)
            zo[1, rows] = near_part(zi[0, rows], piece) + (
                factor_of(zi, 0, heights[piece]) * zi[1, rows]
            )
            send_hop(2, piece)
        returning = pieces(USED)
        for piece in range(2):
            rows = tiles[piece]
            get_hop(2, piece)
            entry = zo[1, rows] + factor_of(zo, 1, heights[piece]) * zi[2, rows]
            for step in ORDER:
                other = lax.rem(y + step, ROW)
                result[other, rows] = (
                    prefix[other, rows] + factor_of(prefix, other, heights[piece]) * entry
                )
                remote(
                    result.at[other, returning[piece]], returned.at[y, returning[piece]],
                    a_send.at[base + 1], a_recv.at[base + 1, 0], (z * ROW + other, head),
                ).start()
            returned[y, rows] = prefix[y, rows] + factor_of(prefix, y, heights[piece]) * entry
        drain(sends)
        whole = pl.ds(0, USED)
        wait_all(result.at[pl.ds(0, ROW - 1), whole], a_send.at[base + 1])
        wait_all(returned.at[pl.ds(0, ROW - 1), whole], a_recv.at[base + 1, 0])

    across(0, up, up_in, USED + 1)


    doc_col = spread(doc_row)
    inside = (sub >= lane) & (doc_col == doc_row)
    enter_col = (doc_col == before).astype(F32)
    leave_col = (doc_col == last).astype(F32)
    loads[4].wait()
    loads[5].wait()
    q_heads = heads_of(q_ref)
    g_heads = heads_of(g_ref)
    for h in range(HEADS):
        row = sums[h : h + 1, :]
        final = row[:, TOK - 1 : TOK]
        col = spread(row)
        qb = q_heads[h].astype(BF16)
        qh[h] = qb
        gh[h] = g_heads[h].astype(BF16)
        qt[h] = jnp.transpose(q_heads[h]) * (jnp.exp(row) * enter_row * FACTOR)
        ent[h] = jnp.exp(col) * enter_col * FACTOR
        leave[h] = jnp.exp(final - col) * leave_col
        weight = jnp.where(inside, jnp.exp(jnp.minimum(col - row, 0.0)), 0.0)
        within[h] = weight
        scores = weight * (nt(qb, kh[h]) * FACTOR)
        score[h] = scores
        out[h] = two(nn, split(scores), vh[h])

    wait_all(up.at[pl.ds(0, ROW - 1), pl.ds(0, USED + 1)], a_send.at[0])
    row_scan(0, True, up_in, part, zout, zin, back, back_in)

    squares = jnp.zeros((TOK, TOK), F32)
    dots = jnp.zeros((TOK, TOK), F32)
    for h in range(HEADS):
        pair = split(unpack(back_in, h))
        state_hi[h] = pair[0]
        state_lo[h] = pair[1]
        now = out[h] + ent[h] * two_right(nn, qh[h], pair)
        out[h] = now
        squares = squares + now * now
        dots = dots + now * gh[h].astype(F32)
    square_row = jnp.sum(jnp.transpose(squares), axis=0, keepdims=True)
    dot_row = jnp.sum(jnp.transpose(dots), axis=0, keepdims=True)
    small = lax.broadcasted_iota(jnp.int32, (8, TOK), 0)
    tile = jnp.where(small == 0, square_row, dot_row)
    hsend[...] = tile
    for step in (4, 5, 3, 6, 2, 7, 1):
        other = lax.rem(head + step, HEAD_DEVS)
        copy = remote(hsend.at[pl.ds(0, 2)], hrecv.at[head, pl.ds(0, 2)], h_send, h_recv, (ctx, other))
        copy.start()
    hrecv[pl.ds(head, 1)] = tile[None]
    for h in range(HEADS):
        pair = split(out[h])
        out_hi[h] = pair[0]
        out_lo[h] = pair[1]
    wait_all(hrecv.at[pl.ds(0, HEAD_DEVS - 1), pl.ds(0, 2)], h_send)
    wait_all(hrecv.at[pl.ds(0, HEAD_DEVS - 1), pl.ds(0, 2)], h_recv)
    total = hrecv[0, 0:2]
    for slot in range(1, HEAD_DEVS):
        total = total + hrecv[slot, 0:2]
    rscale = lax.rsqrt(total[0:1] / FULL + EPS)
    drift = rscale * rscale * rscale * total[1:2] / FULL

    for h in range(HEADS):
        near = split(qt[h] * rscale)
        far = split(qt[h] * drift)
        pulled = two(nn, near, gh[h]) - three(nn, far, (out_hi[h], out_lo[h]))
        pack(pulled, passing[h], 2 * h, upb)

    across(2, upb, upb_in, USED)

    rscale_col = spread(rscale)
    drift_col = spread(drift)
    normed = []
    grads = []
    for h in range(HEADS):
        now = out[h]
        normed.append(now * rscale_col)
        grad_pair = split(rscale_col * gh[h].astype(F32) - drift_col * now)
        mixed = within[h] * two(nt, grad_pair, vh[h])
        grads.append(
            FACTOR * two(nn, split(mixed), kh[h])
            + ent[h] * three(nt, grad_pair, (state_hi[h], state_lo[h]))
        )
        dkl[h] = FACTOR * two(nn, split(jnp.transpose(mixed)), qh[h])
        dvl[h] = three(nn, split(jnp.transpose(score[h])), grad_pair)
    put_heads(att_ref, normed)
    put_heads(dq_ref, grads)

    wait_all(upb.at[pl.ds(0, ROW - 1), pl.ds(0, USED)], a_send.at[2])
    row_scan(2, False, upb_in, partb, zoutb, zinb, backb, backb_in)

    state_pairs = [split(unpack(backb_in, h)) for h in range(HEADS)]
    put_heads(
        dk_ref, [dkl[h] + leave[h] * two_right(nt, vh[h], state_pairs[h]) for h in range(HEADS)]
    )
    put_heads(
        dv_ref, [dvl[h] + leave[h] * two_right(nn, kh[h], state_pairs[h]) for h in range(HEADS)]
    )


def write(*refs):
    srcs, dsts, sem = refs[0:4], refs[4:8], refs[8]
    copies = [pltpu.make_async_copy(a, b, sem.at[n]) for n, (a, b) in enumerate(zip(srcs, dsts))]
    for cut in range(SPLIT):
        rows = pl.ds(TOK // SPLIT * cut, TOK // SPLIT)
        for n, (a, b) in enumerate(zip(srcs, dsts)):
            pltpu.make_async_copy(a.at[rows], b.at[rows], sem.at[n]).start()
    for copy in copies:
        copy.wait()


def local(queries, key_vectors, value_vectors, out_grad, log_decay, doc_ids):
    square_bf = pltpu.VMEM((HEADS, TOK, TOK), BF16)
    square_f = pltpu.VMEM((HEADS, TOK, TOK), F32)
    slices = pltpu.VMEM((ROW, PART, TOK), F32)
    scan = [slices] * 5 + [pltpu.VMEM((2, PART, TOK), F32), pltpu.VMEM((3, PART, TOK), F32)]
    dma = pltpu.SemaphoreType.DMA
    result = jax.ShapeDtypeStruct((TOK, WIDTH), BF16)
    vmem = pl.BlockSpec(memory_space=pltpu.VMEM)
    hbm = pl.BlockSpec(memory_space=pltpu.HBM)
    queries, key_vectors, value_vectors, out_grad, log_decay, docs = (
        pltpu.with_memory_space_constraint(x, pltpu.HBM)
        for x in (
            queries, key_vectors, value_vectors, out_grad, log_decay,
            doc_ids.reshape(ROW * ROWS, TOK),
        )
    )
    results = pl.pallas_call(
        kernel,
        out_shape=[result] * 4,
        in_specs=[hbm] * 6,
        out_specs=[vmem] * 4,
        scratch_shapes=[pltpu.VMEM((TOK, WIDTH), BF16)] * 4
        + [pltpu.VMEM((HEADS, TOK), F32), pltpu.VMEM((8, TOK), jnp.int32), dma((7,))]
        + [square_bf] * 4
        + [square_f] * 6
        + [square_bf] * 4
        + [square_f] * 2
        + scan * 2
        + [pltpu.VMEM((8, TOK), F32), pltpu.VMEM((HEAD_DEVS, 8, TOK), F32)]
        + [dma((4,)), dma((4, 2)), dma((4, 3)), dma((4, 3)), dma, dma],
        compiler_params=pltpu.CompilerParams(
            collective_id=0, has_side_effects=True, vmem_limit_bytes=32 << 20
        ),
    )(
        queries, key_vectors, value_vectors, out_grad, log_decay, docs,
    )
    return pl.pallas_call(
        write,
        out_shape=[result] * 4,
        in_specs=[vmem] * 4,
        out_specs=[hbm] * 4,
        scratch_shapes=[dma((4,))],
    )(*(pltpu.with_memory_space_constraint(x, pltpu.VMEM) for x in results))


def solution(mesh):
    return jax.shard_map(
        local,
        mesh=mesh,
        in_specs=(
            P("ctx", "head"), P("ctx", "head"), P("ctx", "head"), P("ctx", "head"),
            P("head", "ctx"), P(),
        ),
        out_specs=(P("ctx", "head"),) * 4,
        check_vma=False,
    )
```

```python
import jax
import jax.numpy as jnp
from jax import lax
from jax.experimental import pallas as pl
from jax.experimental.pallas import tpu as pltpu
from jax.sharding import PartitionSpec as P

HEADS = 4
DH = 96
TOK = 128
WIDTH = HEADS * DH
FULL = 3072
ROW = 8
ROWS = 12
HEAD_DEVS = 8
PART = 40
USED = 36
SPLIT = 4
CUT = 24
ORDER = (4, 3, 5, 2, 6, 1, 7)
EPS = 1e-05
FACTOR = DH ** (-0.5)
F32 = jnp.float32
BF16 = jnp.bfloat16
MESH = pl.DeviceIdType.MESH


def nn(a, b):
    return lax.dot_general(a, b, (((1,), (0,)), ((), ())), preferred_element_type=F32)


def nt(a, b):
    return lax.dot_general(a, b, (((1,), (1,)), ((), ())), preferred_element_type=F32)


def split(x):
    hi = x.astype(BF16)
    return hi, (x - hi.astype(F32)).astype(BF16)


def two(dot, a, b):
    return dot(a[0], b) + dot(a[1], b)


def two_right(dot, a, b):
    return dot(a, b[0]) + dot(a, b[1])


def three(dot, a, b):
    return dot(a[0], b[0]) + (dot(a[0], b[1]) + dot(a[1], b[0]))


def kernel(
    q_hbm, k_hbm, v_hbm, g_hbm, ld_hbm, doc_hbm,
    att_ref, dq_ref, dk_ref, dv_ref,
    q_ref, k_ref, v_ref, g_ref, ld_ref, doc_ref, in_sem,
    qh, kh, vh, gh, qt, within, score, ent, leave, out, state_hi, state_lo,
    joint, out_lo, dkl, dvl,
    up, up_in, part, back, back_in, zout, zin,
    upb, upb_in, partb, backb, backb_in, zoutb, zinb,
    hsend, hrecv,
    a_send, a_recv, z_send, z_recv, h_send, h_recv,
):
    ctx = lax.axis_index("ctx")
    head = lax.axis_index("head")
    y = lax.rem(ctx, ROW)
    z = ctx // ROW

    def at_row(step):
        return lax.rem(z + step + ROWS, ROWS) * ROW + y

    barrier = pltpu.get_barrier_semaphore()
    for step in ORDER:
        pl.semaphore_signal(
            barrier, inc=1, device_id=(z * ROW + lax.rem(y + step, ROW), head), device_id_type=MESH
        )
    for step in (-2, -1, 1, 2):

        @pl.when((z + step >= 0) & (z + step < ROWS))
        def _(step=step):
            pl.semaphore_signal(barrier, inc=1, device_id=(at_row(step), head), device_id_type=MESH)

    for step in range(1, HEAD_DEVS):
        pl.semaphore_signal(
            barrier, inc=1, device_id=(ctx, lax.rem(head + step, HEAD_DEVS)), device_id_type=MESH
        )

    loads = [
        pltpu.make_async_copy(src, dst, in_sem.at[n])
        for n, (src, dst) in enumerate((
            (ld_hbm, ld_ref), (doc_hbm.at[pl.ds(ctx, 1)], doc_ref.at[pl.ds(1, 1)]),
            (k_hbm, k_ref), (v_hbm, v_ref), (q_hbm, q_ref), (g_hbm, g_ref),
            (doc_hbm.at[pl.ds(jnp.maximum(ctx - 1, 0), 1)], doc_ref.at[pl.ds(0, 1)]),
        ))
    ]
    for n in (0, 1, 6):
        loads[n].start()
    for n, (src, dst) in enumerate(((k_hbm, k_ref), (v_hbm, v_ref), (q_hbm, q_ref), (g_hbm, g_ref))):
        for cut in range(SPLIT):
            rows = pl.ds(TOK // SPLIT * cut, TOK // SPLIT)
            pltpu.make_async_copy(src.at[rows], dst.at[rows], in_sem.at[n + 2]).start()

    lane = lax.broadcasted_iota(jnp.int32, (TOK, TOK), 1)
    sub = lax.broadcasted_iota(jnp.int32, (TOK, TOK), 0)
    real = lane < DH
    data = lax.broadcasted_iota(jnp.int32, (PART - CUT, TOK), 0) < USED - CUT
    wide = lax.broadcasted_iota(jnp.int32, (72, TOK), 1) < DH
    third = lax.broadcasted_iota(jnp.int32, (24, TOK), 1)
    low = lax.broadcasted_iota(jnp.int32, (8, TOK), 0) < 4

    def heads_of(ref):
        tiles = [ref[:, TOK * t : TOK * t + TOK].astype(F32) for t in range(3)]
        zero = jnp.zeros((TOK, TOK), F32)
        h0 = tiles[0]
        h1 = pltpu.roll(jnp.where(lane >= 96, tiles[0], tiles[1]), 32, 1)
        h2 = pltpu.roll(jnp.where(lane >= 64, tiles[1], tiles[2]), 64, 1)
        h3 = pltpu.roll(tiles[2], 96, 1)
        return [jnp.where(real, h, zero) for h in (h0, h1, h2, h3)]

    def put_heads(ref, parts):
        r1 = pltpu.roll(parts[1], 96, 1)
        r2 = pltpu.roll(parts[2], 64, 1)
        r3 = pltpu.roll(parts[3], 32, 1)
        ref[:, 0:TOK] = jnp.where(lane < 96, parts[0], r1).astype(BF16)
        ref[:, TOK : 2 * TOK] = jnp.where(lane < 64, r1, r2).astype(BF16)
        ref[:, 2 * TOK : 3 * TOK] = jnp.where(lane < 32, r2, r3).astype(BF16)

    def spread(row):
        return jnp.transpose(jnp.broadcast_to(row, (TOK, TOK)))

    loads[0].wait()
    loads[1].wait()
    loads[6].wait()
    upper = (sub <= lane).astype(F32)
    sums = lax.dot_general(
        ld_ref[...], upper, (((1,), (0,)), ((), ())),
        precision=lax.Precision.HIGHEST, preferred_element_type=F32,
    )
    doc_row = doc_ref[1:2, :].astype(F32)
    earlier = doc_ref[0:1, TOK - 1 : TOK].astype(F32)
    before = jnp.where(ctx > 0, earlier, -1.0)
    last = doc_row[:, TOK - 1 : TOK]
    enter_row = (doc_row == before).astype(F32)
    leave_row = (doc_row == last).astype(F32)
    through = (last == before).astype(F32)

    def pack(state, decay, slot, dest):
        tail = state[72:96]
        rest = jnp.concatenate(
            [pltpu.roll(tail, 96, 1), pltpu.roll(tail, 64, 1), pltpu.roll(tail, 32, 1)], axis=0
        )
        full = jnp.where(wide, state[0:72], rest)
        dest[slot, 0:32] = full[0:32]
        dest[slot, 32:40] = jnp.where(low, full[32:40], decay)
        dest[slot + 1, 0:32] = full[40:72]
        dest[slot + 1, 32:40] = jnp.where(low, pltpu.roll(full[32:40], 4, 0), decay)

    def unpack(arrived, h):
        one, other = arrived[2 * h], arrived[2 * h + 1]
        full = jnp.concatenate(
            [one[0:32], jnp.where(low, one[32:40], pltpu.roll(other[32:40], 4, 0)), other[0:32]], axis=0
        )
        tail = jnp.where(
            third < 32, pltpu.roll(full[0:24], 32, 1),
            jnp.where(third < 64, pltpu.roll(full[24:48], 64, 1), pltpu.roll(full[48:72], 96, 1)),
        )
        tail = jnp.where(third < DH, tail, 0.0)
        return jnp.concatenate(
            [jnp.where(wide, full, 0.0), tail, jnp.zeros((TOK - DH, TOK), F32)], axis=0
        )

    loads[2].wait()
    loads[3].wait()
    k_heads = heads_of(k_ref)
    v_heads = heads_of(v_ref)
    passing = []
    for h in range(HEADS):
        row = sums[h : h + 1, :]
        final = row[:, TOK - 1 : TOK]
        passing.append(jnp.exp(final) * through)
        vb = v_heads[h].astype(BF16)
        vh[h] = vb
        kh[h] = k_heads[h].astype(BF16)
        kt = jnp.transpose(k_heads[h]) * (jnp.exp(final - row) * leave_row)
        update = two(nn, split(kt), vb)
        pack(update, passing[h], 2 * h, up)

    rows_near = jnp.minimum(z, 2) + jnp.minimum(ROWS - 1 - z, 2)
    pl.semaphore_wait(barrier, (ROW - 1) + (HEAD_DEVS - 1) + rows_near)

    def remote(src, dst, send_sem, recv_sem, target):
        return pltpu.make_async_remote_copy(
            src_ref=src, dst_ref=dst, send_sem=send_sem, recv_sem=recv_sem,
            device_id=target, device_id_type=MESH,
        )

    def wait_all(view, sem):
        pltpu.make_async_copy(view, view, sem).wait()

    def drain(copies):
        for condition, copy in copies:
            if condition is None:
                copy.wait_send()
            else:
                pl.when(condition)(copy.wait_send)

    def pieces(last):
        return (pl.ds(CUT, last - CUT), pl.ds(0, CUT))

    def across(phase, src, dst, last):
        for n, rows in enumerate(pieces(last)):
            for step in ORDER:
                other = lax.rem(y + step, ROW)
                remote(
                    src.at[other, rows], dst.at[y, rows], a_send.at[phase], a_recv.at[phase, n],
                    (z * ROW + other, head),
                ).start()
        dst[pl.ds(y, 1)] = src[pl.ds(y, 1)]

    def factor_of(ref, place, rows):
        return jnp.broadcast_to(ref[place, USED : USED + 1], (rows, TOK))

    def row_scan(base, forward, arrived, prefix, zo, zi, result, returned):
        order = range(ROW) if forward else range(ROW - 1, -1, -1)
        sign = 1 if forward else -1
        place_z = z if forward else ROWS - 1 - z
        sending = (place_z < ROWS - 1, place_z < ROWS - 2, (place_z > 0) & (place_z < ROWS - 2))
        spans = pieces(USED + 1)
        tiles = (slice(CUT, PART), slice(0, CUT))
        heights = (PART - CUT, CUT)
        sends = []

        def hop(n, piece):
            distance = 1 if n == 0 else 2
            return remote(
                zo.at[n // 2, spans[piece]], zi.at[n, spans[piece]],
                z_send.at[base + piece, n], z_recv.at[base + piece, n],
                (at_row(sign * distance), head),
            )

        def send_hop(n, piece):
            copy = hop(n, piece)
            pl.when(sending[n])(copy.start)
            sends.append((sending[n], copy))

        def get_hop(n, piece):
            pl.when(place_z > n)(hop(n, piece).wait_recv)

        def near_part(tile, piece):
            return jnp.where(data, tile, 0.0) if piece == 0 else tile

        for n in range(3):

            @pl.when(place_z <= n)
            def _(n=n):
                zi[n] = jnp.zeros((PART, TOK), F32)

        for piece in range(2):
            rows = tiles[piece]
            count = (USED + 1 if forward else USED) - CUT if piece == 0 else CUT
            wait_all(
                arrived.at[pl.ds(0, ROW - 1), pl.ds(CUT if piece == 0 else 0, count)],
                a_recv.at[base, piece],
            )
            running = jnp.where(data, 0.0, 1.0) if piece == 0 else jnp.zeros((CUT, TOK), F32)
            for place in order:
                prefix[place, rows] = running
                running = near_part(arrived[place, rows], piece) + (
                    factor_of(up_in, place, heights[piece]) * running
                )
            zo[0, rows] = running
            send_hop(1, piece)
            send_hop(0, piece)
        for piece in range(2):
            rows = tiles[piece]
            get_hop(0, piece)
            get_hop(1, piece)
            zo[1, rows] = near_part(zi[0, rows], piece) + (
                factor_of(zi, 0, heights[piece]) * zi[1, rows]
            )
            send_hop(2, piece)
        returning = pieces(USED)
        for piece in range(2):
            rows = tiles[piece]
            get_hop(2, piece)
            entry = zo[1, rows] + factor_of(zo, 1, heights[piece]) * zi[2, rows]
            for step in ORDER:
                other = lax.rem(y + step, ROW)
                result[other, rows] = (
                    prefix[other, rows] + factor_of(prefix, other, heights[piece]) * entry
                )
                remote(
                    result.at[other, returning[piece]], returned.at[y, returning[piece]],
                    a_send.at[base + 1], a_recv.at[base + 1, 0], (z * ROW + other, head),
                ).start()
            returned[y, rows] = prefix[y, rows] + factor_of(prefix, y, heights[piece]) * entry
        drain(sends)
        whole = pl.ds(0, USED)
        wait_all(result.at[pl.ds(0, ROW - 1), whole], a_send.at[base + 1])
        wait_all(returned.at[pl.ds(0, ROW - 1), whole], a_recv.at[base + 1, 0])

    across(0, up, up_in, USED + 1)


    doc_col = spread(doc_row)
    inside = (sub >= lane) & (doc_col == doc_row)
    enter_col = (doc_col == before).astype(F32)
    leave_col = (doc_col == last).astype(F32)
    loads[4].wait()
    loads[5].wait()
    q_heads = heads_of(q_ref)
    g_heads = heads_of(g_ref)
    for h in range(HEADS):
        row = sums[h : h + 1, :]
        final = row[:, TOK - 1 : TOK]
        col = spread(row)
        qb = q_heads[h].astype(BF16)
        qh[h] = qb
        gh[h] = g_heads[h].astype(BF16)
        qt[h] = jnp.transpose(q_heads[h]) * (jnp.exp(row) * enter_row * FACTOR)
        ent[h] = jnp.exp(col) * enter_col * FACTOR
        leave[h] = jnp.exp(final - col) * leave_col
        weight = jnp.where(inside, jnp.exp(jnp.minimum(col - row, 0.0)), 0.0)
        within[h] = weight
        scores = weight * (nt(qb, kh[h]) * FACTOR)
        score[h] = scores
        out[h] = two(nn, split(scores), vh[h])

    wait_all(up.at[pl.ds(0, ROW - 1), pl.ds(0, USED + 1)], a_send.at[0])
    row_scan(0, True, up_in, part, zout, zin, back, back_in)

    squares = jnp.zeros((TOK, TOK), F32)
    dots = jnp.zeros((TOK, TOK), F32)
    for h in range(HEADS):
        pair = split(unpack(back_in, h))
        state_hi[h] = pair[0]
        state_lo[h] = pair[1]
        now = out[h] + ent[h] * two_right(nn, qh[h], pair)
        out[h] = now
        squares = squares + now * now
        dots = dots + now * gh[h].astype(F32)
    square_row = jnp.sum(jnp.transpose(squares), axis=0, keepdims=True)
    dot_row = jnp.sum(jnp.transpose(dots), axis=0, keepdims=True)
    small = lax.broadcasted_iota(jnp.int32, (8, TOK), 0)
    tile = jnp.where(small == 0, square_row, dot_row)
    hsend[...] = tile
    for step in (4, 5, 3, 6, 2, 7, 1):
        other = lax.rem(head + step, HEAD_DEVS)
        copy = remote(hsend.at[pl.ds(0, 2)], hrecv.at[head, pl.ds(0, 2)], h_send, h_recv, (ctx, other))
        copy.start()
    hrecv[pl.ds(head, 1)] = tile[None]
    for h in range(HEADS):
        pair = split(out[h])
        joint[h, 0:TOK] = gh[h]
        joint[h, TOK : 2 * TOK] = pair[0]
        out_lo[h] = pair[1]
    wait_all(hrecv.at[pl.ds(0, HEAD_DEVS - 1), pl.ds(0, 2)], h_send)
    wait_all(hrecv.at[pl.ds(0, HEAD_DEVS - 1), pl.ds(0, 2)], h_recv)
    total = hrecv[0, 0:2]
    for slot in range(1, HEAD_DEVS):
        total = total + hrecv[slot, 0:2]
    rscale = lax.rsqrt(total[0:1] / FULL + EPS)
    drift = rscale * rscale * rscale * total[1:2] / FULL

    for h in range(HEADS):
        left = split(jnp.concatenate([qt[h] * rscale, qt[h] * -drift], axis=1))
        pulled = two(nn, left, joint[h]) + nn(left[0][:, TOK : 2 * TOK], out_lo[h])
        pack(pulled, passing[h], 2 * h, upb)

    across(2, upb, upb_in, USED)

    rscale_col = spread(rscale)
    drift_col = spread(drift)
    normed = []
    grads = []
    for h in range(HEADS):
        now = out[h]
        normed.append(now * rscale_col)
        grad_pair = split(rscale_col * gh[h].astype(F32) - drift_col * now)
        mixed = within[h] * two(nt, grad_pair, vh[h])
        grads.append(
            FACTOR * two(nn, split(mixed), kh[h])
            + ent[h] * three(nt, grad_pair, (state_hi[h], state_lo[h]))
        )
        dkl[h] = FACTOR * two(nn, split(jnp.transpose(mixed)), qh[h])
        dvl[h] = three(nn, split(jnp.transpose(score[h])), grad_pair)
    put_heads(att_ref, normed)
    put_heads(dq_ref, grads)

    wait_all(upb.at[pl.ds(0, ROW - 1), pl.ds(0, USED)], a_send.at[2])
    row_scan(2, False, upb_in, partb, zoutb, zinb, backb, backb_in)

    state_pairs = [split(unpack(backb_in, h)) for h in range(HEADS)]
    put_heads(
        dk_ref, [dkl[h] + leave[h] * two_right(nt, vh[h], state_pairs[h]) for h in range(HEADS)]
    )
    put_heads(
        dv_ref, [dvl[h] + leave[h] * two_right(nn, kh[h], state_pairs[h]) for h in range(HEADS)]
    )


def write(*refs):
    srcs, dsts, sem = refs[0:4], refs[4:8], refs[8]
    copies = [pltpu.make_async_copy(a, b, sem.at[n]) for n, (a, b) in enumerate(zip(srcs, dsts))]
    for cut in range(SPLIT):
        rows = pl.ds(TOK // SPLIT * cut, TOK // SPLIT)
        for n, (a, b) in enumerate(zip(srcs, dsts)):
            pltpu.make_async_copy(a.at[rows], b.at[rows], sem.at[n]).start()
    for copy in copies:
        copy.wait()


def local(queries, key_vectors, value_vectors, out_grad, log_decay, doc_ids):
    square_bf = pltpu.VMEM((HEADS, TOK, TOK), BF16)
    square_f = pltpu.VMEM((HEADS, TOK, TOK), F32)
    slices = pltpu.VMEM((ROW, PART, TOK), F32)
    scan = [slices] * 5 + [pltpu.VMEM((2, PART, TOK), F32), pltpu.VMEM((3, PART, TOK), F32)]
    dma = pltpu.SemaphoreType.DMA
    result = jax.ShapeDtypeStruct((TOK, WIDTH), BF16)
    vmem = pl.BlockSpec(memory_space=pltpu.VMEM)
    hbm = pl.BlockSpec(memory_space=pltpu.HBM)
    queries, key_vectors, value_vectors, out_grad, log_decay, docs = (
        pltpu.with_memory_space_constraint(x, pltpu.HBM)
        for x in (
            queries, key_vectors, value_vectors, out_grad, log_decay,
            doc_ids.reshape(ROW * ROWS, TOK),
        )
    )
    results = pl.pallas_call(
        kernel,
        out_shape=[result] * 4,
        in_specs=[hbm] * 6,
        out_specs=[vmem] * 4,
        scratch_shapes=[pltpu.VMEM((TOK, WIDTH), BF16)] * 4
        + [pltpu.VMEM((HEADS, TOK), F32), pltpu.VMEM((8, TOK), jnp.int32), dma((7,))]
        + [square_bf] * 4
        + [square_f] * 6
        + [square_bf] * 2
        + [pltpu.VMEM((HEADS, 2 * TOK, TOK), BF16), square_bf]
        + [square_f] * 2
        + scan * 2
        + [pltpu.VMEM((8, TOK), F32), pltpu.VMEM((HEAD_DEVS, 8, TOK), F32)]
        + [dma((4,)), dma((4, 2)), dma((4, 3)), dma((4, 3)), dma, dma],
        compiler_params=pltpu.CompilerParams(
            collective_id=0, has_side_effects=True, vmem_limit_bytes=32 << 20
        ),
    )(
        queries, key_vectors, value_vectors, out_grad, log_decay, docs,
    )
    return pl.pallas_call(
        write,
        out_shape=[result] * 4,
        in_specs=[vmem] * 4,
        out_specs=[hbm] * 4,
        scratch_shapes=[dma((4,))],
    )(*(pltpu.with_memory_space_constraint(x, pltpu.VMEM) for x in results))


def solution(mesh):
    return jax.shard_map(
        local,
        mesh=mesh,
        in_specs=(
            P("ctx", "head"), P("ctx", "head"), P("ctx", "head"), P("ctx", "head"),
            P("head", "ctx"), P(),
        ),
        out_specs=(P("ctx", "head"),) * 4,
        check_vma=False,
    )
```
